32 devices in a mesh: seq: 16 (over z, y, x), head: 2 (over core).
Axes of the slice: x: 2, y: 2, z: 4, core: 2. Of those that a mesh axis runs over, the one named last changes fastest.
Arguments:
- query_elements: bfloat16 [16384, 4096], P('seq', 'head'), may hold values from -4 to 4
- query_exponents: int32 [16384, 128], P('seq', 'head'), may hold values from -1 to 1
- key_elements: bfloat16 [16384, 512], P('seq', 'head'), may hold values from -4 to 4
- key_exponents: int32 [16384, 16], P('seq', 'head'), may hold values from -1 to 1
- value_elements: bfloat16 [16384, 512], P('seq', 'head'), may hold values from -4 to 4
- value_exponents: int32 [16384, 16], P('seq', 'head'), may hold values from -1 to 1
- query_clip_words: int32 [16384, 256], P('seq', 'head'), may hold values from 0 to 65280, as said below
- key_clip_words: int32 [16384, 32], P('seq', 'head'), may hold values from 0 to 65280, as said below
- sinks: float32 [64], P('head'), may hold values from -2 to 2
- rotation: float32 [8, 64, 64], P('head'), may hold values from -0.75 to 0.75
- output_gradient: bfloat16 [16384, 4096], P('seq', 'head'), may hold values from -120 to 120
Outputs:
- grad_q: bfloat16 [16384, 4096], P('seq', 'head')
- key_gradient_raw: bfloat16 [16384, 512], P('seq', 'head')
- value_gradient: bfloat16 [16384, 512], P('seq', 'head')
- grad_rotation: float32 [8, 64, 64], P('head')
- grad_sinks: float32 [64], P('head')
The draws below stay inside these ranges and needn't reach their ends.
Inputs may be any that keep to these rules, and one draw needn't show every extreme that they name: `query_clip_words`: bit b of word w of a row is 1 where entry 16 w + b of the row passed the clip; a word whose upper eight bits are all set has its lower eight bits clear. `key_clip_words`: bit b of word w of a row is 1 where entry 16 w + b of the row passed the clip; a word whose upper eight bits are all set has its lower eight bits clear.
All inputs are finite; a program needn't handle non-finite values.
Results may differ from the reference program's by a relative error of at most 0.0097.
Values may be sent and summed in bfloat16 or wider, within the bound.
No kernel may reach another device: no remote copies, remote signals or barrier semaphores. Data moves between devices by JAX's collectives and lax.ppermute only.
A program may use at most 128 MiB of HBM per device.

```python
import math
import jax
import jax.numpy as jnp
from jax import lax

HEAD_ENTRIES = 64
KEY_VALUE_HEADS = 8
QUERY_PER_GROUP = 8
WINDOW = 128
SHARED_EXPONENT = 32
HQ = 64
SEQUENCE_TOKENS = 16384


def draw_query_elements(key, part):
    local_key = jax.random.fold_in(key, 11)
    final_result = jnp.clip(jax.random.normal(local_key, (SEQUENCE_TOKENS, HQ * HEAD_ENTRIES), jnp.float32), -4.0, 4.0)
    return final_result.astype(jnp.bfloat16)


def draw_key_elements(key, part):
    local_key = jax.random.fold_in(key, 12)
    final_result = jnp.clip(jax.random.normal(local_key, (SEQUENCE_TOKENS, KEY_VALUE_HEADS * HEAD_ENTRIES), jnp.float32), -4.0, 4.0)
    return final_result.astype(jnp.bfloat16)


def draw_output_gradient(key, part):
    positions = jnp.arange(SEQUENCE_TOKENS, dtype=jnp.float32)
    head_list = jnp.arange(HQ * HEAD_ENTRIES, dtype=jnp.int32) // HEAD_ENTRIES
    head_groups = (head_list // QUERY_PER_GROUP).astype(jnp.float32)
    head_spreading = 10.0 ** (0.5 * jax.random.uniform(jax.random.fold_in(key, 21), (HQ,), jnp.float32))
    column_factor = 3.0 ** (head_groups / max(KEY_VALUE_HEADS - 1, 1)) * head_spreading[head_list]
    row_scale = 3.0 ** (positions / max(SEQUENCE_TOKENS - 1, 1))
    local_key = jax.random.fold_in(key, 22)
    base_values = jnp.clip(jax.random.normal(local_key, (SEQUENCE_TOKENS, HQ * HEAD_ENTRIES), jnp.float32), -4.0, 4.0)
    return (base_values * row_scale[:, None] * column_factor[None, :]).astype(jnp.bfloat16)


def capped_flags(key, first_tag, second_tag, width):
    first_bits = jax.random.randint(jax.random.fold_in(key, first_tag), (SEQUENCE_TOKENS, width), 0, 65536, dtype=jnp.int32)
    second_bits = jax.random.randint(jax.random.fold_in(key, second_tag), (SEQUENCE_TOKENS, width), 0, 65536, dtype=jnp.int32)
    joined = jnp.bitwise_or(first_bits, second_bits)
    upper_full = jnp.bitwise_and(joined, 65280) == 65280
    return jnp.where(upper_full, jnp.bitwise_and(joined, 65280), joined)


def draw_query_clip_words(key, part):
    return capped_flags(key, 31, 32, HQ * HEAD_ENTRIES // 16)


def draw_key_clip_words(key, part):
    return capped_flags(key, 41, 42, KEY_VALUE_HEADS * HEAD_ENTRIES // 16)


def place_ends(drawn, key, least, largest):
    extent = drawn.shape
    place = [jax.random.randint(jax.random.fold_in(key, axis), (), 0, extent[axis]) for axis in range(len(extent))]
    drawn = drawn.at[tuple(place)].set(least)
    longest = extent.index(max(extent))
    place[longest] = (place[longest] + 1) % extent[longest]
    return drawn.at[tuple(place)].set(largest)


def levels(stream_key, extent, split, low, largest):
    level = 1.0
    for axis_at, shards_of in split:
        steps = jax.random.uniform(jax.random.fold_in(jax.random.fold_in(stream_key, 6), axis_at), (shards_of,), jnp.float32, low / len(split), largest / len(split))
        level = level * jnp.repeat(jnp.exp(steps), extent[axis_at] // shards_of).reshape((-1,) + (1,) * (len(extent) - 1 - axis_at))
    return level


def noise(rng, shape, scale, bound, pieces=(), held_as=jnp.bfloat16):
    array = scale * jax.random.normal(rng, shape, jnp.float32)
    if pieces:
        array = array * levels(rng, shape, pieces, -0.22, 0.18)
    return jnp.clip(array, -bound, bound).astype(held_as)


def setup_inputs(seed: int = 0) -> dict:
    key_list = jax.random.split(jax.random.key(seed), 12)
    query_elements = draw_query_elements(jax.random.fold_in(key_list[11], 71), 0)
    query_exponents = place_ends(jax.random.randint(key_list[1], (SEQUENCE_TOKENS, HQ * HEAD_ENTRIES // SHARED_EXPONENT), -1, 2), jax.random.fold_in(key_list[1], 1), -1, 1).astype(jnp.int32)
    key_elements = draw_key_elements(jax.random.fold_in(key_list[11], 71), 0)
    key_exponents = place_ends(jax.random.randint(key_list[3], (SEQUENCE_TOKENS, KEY_VALUE_HEADS * HEAD_ENTRIES // SHARED_EXPONENT), -1, 2), jax.random.fold_in(key_list[3], 1), -1, 1).astype(jnp.int32)
    value_elements = noise(key_list[4], (SEQUENCE_TOKENS, KEY_VALUE_HEADS * HEAD_ENTRIES), 1.0, 4.0, ((0, 16), (1, 2)))
    value_exponents = place_ends(jax.random.randint(key_list[5], (SEQUENCE_TOKENS, KEY_VALUE_HEADS * HEAD_ENTRIES // SHARED_EXPONENT), -1, 2), jax.random.fold_in(key_list[5], 1), -1, 1).astype(jnp.int32)
    query_clip_words = draw_query_clip_words(jax.random.fold_in(key_list[11], 71), 0)
    key_clip_words = draw_key_clip_words(jax.random.fold_in(key_list[11], 71), 0)
    sinks = jnp.clip(jax.random.uniform(key_list[8], (HQ,), jnp.float32, -2.0, 2.0) * levels(key_list[8], (HQ,), ((0, 2),), -0.4, 0.0), -2.0, 2.0)
    rotation = noise(key_list[9], (KEY_VALUE_HEADS, HEAD_ENTRIES, HEAD_ENTRIES), HEAD_ENTRIES ** -0.5, 0.75, ((0, 2),), jnp.float32)
    output_gradient = draw_output_gradient(jax.random.fold_in(key_list[11], 71), 0)
    return dict(query_elements=query_elements, query_exponents=query_exponents, key_elements=key_elements, key_exponents=key_exponents, value_elements=value_elements, value_exponents=value_exponents, query_clip_words=query_clip_words, key_clip_words=key_clip_words, sinks=sinks, rotation=rotation, output_gradient=output_gradient)


clip_scale = 64.0
limit_factor = 0.05
negative = -1e+30

def decode_blocks(element_vals, powers):
    row_count = element_vals.shape[0]
    scaled = element_vals.astype(jnp.float32).reshape(row_count, -1, SHARED_EXPONENT) * jnp.exp2(powers.astype(jnp.float32))[:, :, None]
    return scaled.reshape(row_count, -1).astype(jnp.bfloat16)

def unpack_words(packed):
    shifts = jnp.arange(16, dtype=jnp.int32)
    bit_vals = jnp.right_shift(packed[:, :, None], shifts[None, None, :]) & 1
    return bit_vals.reshape(packed.shape[0], -1).astype(jnp.float32)

def attend(query_blk, dout_blk, keys_blk, values, sink_logit, query_pos, key_pos):
    temper = HEAD_ENTRIES ** (-0.5)
    query_f = query_blk.astype(jnp.float32)
    dout_f = dout_blk.astype(jnp.float32)
    keys_f = keys_blk.astype(jnp.float32)
    values_f = values.astype(jnp.float32)
    scores = jnp.einsum('iqd,jd->qij', query_f, keys_f) * temper
    allowed = (key_pos[None, :] <= query_pos[:, None]) & (key_pos[None, :] > query_pos[:, None] - WINDOW) & (key_pos[None, :] >= 0)
    scores = jnp.where(allowed[None], scores, negative)
    row_max = jnp.maximum(lax.optimization_barrier(jnp.max(scores, axis=2)), sink_logit[:, None])
    numerators = jnp.where(allowed[None], jnp.exp(scores - row_max[:, :, None]), 0.0)
    totals = lax.optimization_barrier(jnp.sum(numerators, axis=2)) + jnp.exp(sink_logit[:, None] - row_max)
    weights = numerators / totals[:, :, None]
    rounded = weights.astype(jnp.bfloat16).astype(jnp.float32)
    outputs = jnp.einsum('qij,jd->iqd', rounded, values_f)
    deltas = lax.optimization_barrier(jnp.sum(dout_f * outputs, axis=2)).T
    grad_probs = jnp.einsum('iqd,jd->qij', dout_f, values_f)
    grad_scores = (weights * (grad_probs - deltas[:, :, None])).astype(jnp.bfloat16).astype(jnp.float32)
    grad_query = jnp.einsum('qij,jd->iqd', grad_scores, keys_f) * temper
    grad_keys = jnp.einsum('qij,iqd->jd', grad_scores, query_f) * temper
    grad_vals = jnp.einsum('qij,iqd->jd', rounded, dout_f)
    sink_terms = -lax.optimization_barrier(jnp.sum(jnp.exp(sink_logit[:, None] - row_max) / totals * deltas, axis=1))
    return (grad_query, grad_keys, grad_vals, sink_terms)

def reference(query_elements, query_exponents, key_elements, key_exponents, value_elements, value_exponents, query_clip_words, key_clip_words, sinks, rotation, output_gradient):
    query_rows_list = decode_blocks(query_elements, query_exponents).reshape(SEQUENCE_TOKENS, KEY_VALUE_HEADS, QUERY_PER_GROUP, HEAD_ENTRIES).transpose(1, 0, 2, 3)
    key_row_list = decode_blocks(key_elements, key_exponents).reshape(SEQUENCE_TOKENS, KEY_VALUE_HEADS, HEAD_ENTRIES).transpose(1, 0, 2)
    value_row_list = decode_blocks(value_elements, value_exponents).reshape(SEQUENCE_TOKENS, KEY_VALUE_HEADS, HEAD_ENTRIES).transpose(1, 0, 2)
    output_grad_list = output_gradient.reshape(SEQUENCE_TOKENS, KEY_VALUE_HEADS, QUERY_PER_GROUP, HEAD_ENTRIES).transpose(1, 0, 2, 3)
    query_flags = unpack_words(query_clip_words).reshape(SEQUENCE_TOKENS, KEY_VALUE_HEADS, QUERY_PER_GROUP, HEAD_ENTRIES).transpose(1, 0, 2, 3)
    key_flags = unpack_words(key_clip_words).reshape(SEQUENCE_TOKENS, KEY_VALUE_HEADS, HEAD_ENTRIES).transpose(1, 0, 2)
    sink_row_list = sinks.reshape(KEY_VALUE_HEADS, QUERY_PER_GROUP)
    block_count = SEQUENCE_TOKENS // WINDOW

    def group(items):
        query_g, key_g, value_g, dout_g, qbit_g, kbit_g, sink_g, rot_g = items
        zero_rows = jnp.zeros((WINDOW, HEAD_ENTRIES), jnp.bfloat16)
        key_pad = jnp.concatenate([zero_rows, key_g], 0)
        value_pad = jnp.concatenate([zero_rows, value_g], 0)

        def block(block_index):
            begin_row = block_index * WINDOW
            query_b = lax.dynamic_slice_in_dim(query_g, begin_row, WINDOW, 0)
            dout_b = lax.dynamic_slice_in_dim(dout_g, begin_row, WINDOW, 0)
            keys_b = lax.dynamic_slice_in_dim(key_pad, begin_row, 2 * WINDOW, 0)
            values_b = lax.dynamic_slice_in_dim(value_pad, begin_row, 2 * WINDOW, 0)
            query_pos = begin_row + jnp.arange(WINDOW, dtype=jnp.int32)
            key_pos = begin_row - WINDOW + jnp.arange(2 * WINDOW, dtype=jnp.int32)
            return attend(query_b, dout_b, keys_b, values_b, sink_g, query_pos, key_pos)
        grad_query, grad_keys, grad_vals, sink_terms = lax.map(block, jnp.arange(block_count, dtype=jnp.int32))
        zero_tail = jnp.zeros((1, WINDOW, HEAD_ENTRIES), jnp.float32)
        key_total = grad_keys[:, WINDOW:] + jnp.concatenate([grad_keys[1:, :WINDOW], zero_tail], 0)
        value_total = grad_vals[:, WINDOW:] + jnp.concatenate([grad_vals[1:, :WINDOW], zero_tail], 0)
        grad_query = grad_query.reshape(SEQUENCE_TOKENS, QUERY_PER_GROUP, HEAD_ENTRIES)
        key_total = key_total.reshape(SEQUENCE_TOKENS, HEAD_ENTRIES)
        value_total = value_total.reshape(SEQUENCE_TOKENS, HEAD_ENTRIES)
        masked_query = (grad_query * qbit_g).astype(jnp.bfloat16)
        masked_keys = (key_total * kbit_g).astype(jnp.bfloat16)
        rotation_low = rot_g.astype(jnp.bfloat16)
        grad_query_pre = jnp.einsum('tqd,ed->tqe', masked_query.astype(jnp.float32), rotation_low.astype(jnp.float32)).astype(jnp.bfloat16)
        grad_key_pre = jnp.dot(masked_keys, rotation_low.T, preferred_element_type=jnp.float32).astype(jnp.bfloat16)
        partial_value = jnp.dot(query_g.reshape(-1, HEAD_ENTRIES).T, masked_query.reshape(-1, HEAD_ENTRIES), preferred_element_type=jnp.float32)
        partial_value = partial_value + jnp.dot(key_g.T, masked_keys, preferred_element_type=jnp.float32)
        raw_grad = jnp.dot(rot_g, partial_value, precision=lax.Precision.HIGHEST)
        return (grad_query_pre, grad_key_pre, value_total.astype(jnp.bfloat16), raw_grad, lax.optimization_barrier(jnp.sum(sink_terms, axis=0)))
    grad_query_all, every_key_gradient, every_value_gradient, raw_all, sink_all = lax.map(group, (query_rows_list, key_row_list, value_row_list, output_grad_list, query_flags, key_flags, sink_row_list, rotation))
    limit_value = limit_factor * math.sqrt(SEQUENCE_TOKENS * HQ * HEAD_ENTRIES)
    norm_value = jnp.sqrt(jnp.sum(raw_all * raw_all))
    grad_rotation = raw_all * (clip_scale / jnp.maximum(norm_value, limit_value))
    grad_q = grad_query_all.transpose(1, 0, 2, 3).reshape(SEQUENCE_TOKENS, HQ * HEAD_ENTRIES)
    key_gradient_raw = every_key_gradient.transpose(1, 0, 2).reshape(SEQUENCE_TOKENS, KEY_VALUE_HEADS * HEAD_ENTRIES)
    value_gradient = every_value_gradient.transpose(1, 0, 2).reshape(SEQUENCE_TOKENS, KEY_VALUE_HEADS * HEAD_ENTRIES)
    return (grad_q, key_gradient_raw, value_gradient, grad_rotation, sink_all.reshape(HQ))
```

```python
import functools
import math

import jax
import jax.numpy as jnp
from jax import lax
from jax.experimental import pallas as pl
from jax.experimental.pallas import tpu as pltpu
from jax.sharding import PartitionSpec as P

WINDOW = 128
SHARED_EXPONENT = 32
WORD_BITS = 16
LANES = 128
ROWS = 64
BAND = WINDOW + ROWS

clip_scale = 64.0
limit_factor = 0.05
negative = -1e30

f32 = jnp.float32
bf16 = jnp.bfloat16
i32 = jnp.int32


def iota(shape, dim):
    return lax.broadcasted_iota(i32, shape, dim)


def mm(a, b):
    return lax.dot_general(a, b, (((1,), (0,)), ((), ())), preferred_element_type=f32)


def mm_nt(a, b):
    return lax.dot_general(a, b, (((1,), (1,)), ((), ())), preferred_element_type=f32)


def mm_tn(a, b):
    return lax.dot_general(a, b, (((0,), (0,)), ((), ())), preferred_element_type=f32)


def decoded(elements, powers):
    width = elements.shape[1]
    shape = (powers.shape[1], width)
    spread = (iota(shape, 1) // SHARED_EXPONENT == iota(shape, 0)).astype(f32).astype(bf16)
    scale = mm(jnp.exp2(powers.astype(f32)).astype(bf16), spread)
    return elements * scale.astype(bf16)


def word_bytes(words):
    count = words.shape[1]
    shape = (count, LANES)
    low = (iota(shape, 1) == iota(shape, 0)).astype(f32).astype(bf16)
    high = (iota(shape, 1) == iota(shape, 0) + count).astype(f32).astype(bf16)
    first = (words & 255).astype(f32).astype(bf16)
    second = ((words >> 8) & 255).astype(f32).astype(bf16)
    return (mm(first, low) + mm(second, high)).astype(bf16)


def byte_flags(byte_rows, width):
    count = width // WORD_BITS
    shape = (LANES, width)
    lane, row = iota(shape, 1), iota(shape, 0)
    word = lane // WORD_BITS
    upper = (lane % WORD_BITS) // 8
    spread = (row == word + upper * count).astype(f32).astype(bf16)
    value = mm(byte_rows, spread).astype(i32)
    bit = jnp.left_shift(jnp.ones(value.shape, i32), iota(value.shape, 1) % 8)
    return (value & bit) != 0


def halo_kernel(k_ref, ke_ref, v_ref, ve_ref, w_ref, out_ref):
    width = k_ref.shape[1]
    out_ref[:, :width] = decoded(k_ref[...], ke_ref[...])
    out_ref[:, width : 2 * width] = decoded(v_ref[...], ve_ref[...])
    out_ref[:, 2 * width :] = word_bytes(w_ref[...])


def main_kernel(
    groups,
    per_group,
    sink_ref,
    q_ref,
    qe_ref,
    do_ref,
    qw_ref,
    k_ref,
    ke_ref,
    v_ref,
    ve_ref,
    kw_ref,
    halo_ref,
    rot_ref,
    gq_ref,
    pay_ref,
    ret_ref,
    dk_ref,
    dv_ref,
    kn,
    kz,
    vz,
    acck,
    accv,
    accp,
    accs,
    sinks,
    lowmask,
):
    b = pl.program_id(0)
    last = pl.num_programs(0) - 1
    width = k_ref.shape[1]
    pairs = width // LANES
    side = per_group // 2
    lanes = side * ROWS
    head = LANES // 2
    first_device = lax.axis_index("seq") == 0

    @pl.when(b == 0)
    def _():
        eighth = jnp.asarray(head**-0.5, bf16)
        kn[:WINDOW] = halo_ref[:, :width] * eighth
        kn[WINDOW:] = decoded(k_ref[...], ke_ref[...]) * eighth
        vals = decoded(v_ref[...], ve_ref[...])
        lane = iota((1, LANES), 1)
        for g in range(groups):
            keep = ((lane // head) == g % 2).astype(f32).astype(bf16)
            at = (g // 2) * LANES
            kz[g] = kn[:, at : at + LANES] * keep
            vz[g, :WINDOW] = halo_ref[:, width + at : width + at + LANES] * keep
            vz[g, WINDOW:] = vals[:, at : at + LANES] * keep
        acck[...] = jnp.zeros_like(acck)
        accv[...] = jnp.zeros_like(accv)
        accp[...] = jnp.zeros_like(accp)
        accs[...] = jnp.zeros_like(accs)
        pairof = iota((1, lanes), 1) // ROWS
        for g in range(groups):
            for odd in range(2):
                row = jnp.zeros((1, lanes), f32)
                for p in range(side):
                    row = jnp.where(pairof == p, sink_ref[g * per_group + 2 * p + odd], row)
                sinks[pl.ds(2 * g + odd, 1), :] = row
        lowmask[...] = (
            (iota((ROWS, lanes), 0) > iota((ROWS, lanes), 1) % ROWS).astype(f32).astype(bf16)
        )

    def body(edge):
        start = pl.multiple_of(b * ROWS, ROWS)
        q = decoded(q_ref[...], qe_ref[...])
        do = do_ref[...]
        words = jnp.transpose(qw_ref[...])
        current = iota((ROWS, lanes), 0) <= iota((ROWS, lanes), 1) % ROWS
        lower = iota((1, LANES), 1) < head
        low = lowmask[...]
        bit = jnp.left_shift(jnp.ones((head, 1), i32), iota((head, 1), 0) % WORD_BITS)
        limit = jnp.where(first_device, WINDOW, 0) - start

        def tiles(rows, g):
            return jnp.concatenate(
                [rows[:, (side * g + p) * LANES : (side * g + p + 1) * LANES] for p in range(side)],
                axis=0,
            )

        def combined(x):
            low_part, mid, high = x[:ROWS], x[ROWS : 2 * ROWS], x[2 * ROWS :]
            return jnp.concatenate([jnp.where(current, high, low_part), mid], axis=0)

        def spread(x):
            first = x[:ROWS] * low
            return jnp.concatenate([first, x[ROWS:], x[:ROWS] - first], axis=0)

        for pair in range(pairs):
            at = pair * LANES
            ktr = jnp.transpose(kn[pl.ds(start, BAND), at : at + LANES])
            sums_k, sums_v, sums_p = [], [], []
            for half in range(2):
                g = 2 * pair + half
                if g >= groups:
                    continue
                kb = kz[g, pl.ds(start, BAND), :]
                vb = vz[g, pl.ds(start, BAND), :]
                aq, ad = tiles(q, g), tiles(do, g)
                bq, bd = pltpu.roll(aq, head, 1), pltpu.roll(ad, head, 1)
                wq, wd = ([aq, bq], [ad, bd]) if half == 0 else ([bq, aq], [bd, ad])
                probs, grads, dqs = [], [], []
                for odd in range(2):
                    scores = mm_nt(kb, wq[odd])
                    if edge:
                        scores = jnp.where(iota((BAND, 1), 0) >= limit, scores, negative)
                    scores = combined(scores)
                    sink = sinks[pl.ds(2 * g + odd, 1), :]
                    row_max = jnp.maximum(jnp.max(scores, axis=0, keepdims=True), sink)
                    numer = jnp.exp(scores - row_max)
                    sink_numer = jnp.exp(sink - row_max)
                    inverse = 1.0 / (jnp.sum(numer, axis=0, keepdims=True) + sink_numer)
                    weights = numer * inverse
                    gprobs = combined(mm_nt(vb, wd[odd]))
                    delta = jnp.sum(weights * gprobs, axis=0, keepdims=True)
                    gscores = (weights * (gprobs - delta)).astype(bf16)
                    accs[pl.ds(2 * g + odd, 1), :] -= sink_numer * inverse * delta
                    probs.append(spread(weights.astype(bf16)))
                    gs = spread(gscores)
                    grads.append(gs)
                    dqs.append(mm(ktr[half * head : (half + 1) * head], gs))
                probs = jnp.concatenate(probs, axis=1)
                grads = jnp.concatenate(grads, axis=1)
                wq = jnp.concatenate(wq, axis=0)
                wd = jnp.concatenate(wd, axis=0)
                sums_k.append(mm(grads, wq))
                sums_v.append(mm(probs, wd))
                per_pair = 2 * head // WORD_BITS
                base = g * side * per_pair
                wcat = jnp.concatenate(
                    [words[base + p * per_pair : base + (p + 1) * per_pair] for p in range(side)],
                    axis=1,
                )
                masked = []
                for odd in range(2):
                    spots = jnp.concatenate(
                        [
                            jnp.broadcast_to(wcat[n : n + 1], (WORD_BITS, lanes))
                            for n in range(odd * per_pair // 2, (odd + 1) * per_pair // 2)
                        ],
                        axis=0,
                    )
                    masked.append(jnp.where((spots & bit) != 0, dqs[odd], 0.0).astype(bf16))
                masked = jnp.concatenate(masked, axis=1)
                sums_p.append(mm(masked, wq))
                turned = mm(rot_ref[g].astype(bf16), masked).astype(bf16)
                turned = jnp.concatenate([turned[:, :lanes], turned[:, lanes:]], axis=0)
                turned = jnp.transpose(turned)
                for p in range(side):
                    cols = (side * g + p) * LANES
                    gq_ref[:, cols : cols + LANES] = turned[p * ROWS : (p + 1) * ROWS]

            def merged(parts):
                other = parts[1] if len(parts) > 1 else 0.0
                return jnp.where(lower, parts[0], other)

            acck[pl.ds(start, BAND), at : at + LANES] += merged(sums_k)
            accv[pl.ds(start, BAND), at : at + LANES] += merged(sums_v)
            accp[pair * head : (pair + 1) * head] += merged(sums_p)

    @pl.when(b < WINDOW // ROWS)
    def _():
        body(True)

    @pl.when(b >= WINDOW // ROWS)
    def _():
        body(False)

    @pl.when(b == last)
    def _():
        scale = head**-0.5
        lower = iota((1, LANES), 1) < head
        bytes_all = jnp.concatenate([halo_ref[:, 2 * width :], word_bytes(kw_ref[...])], axis=0)
        flags = byte_flags(bytes_all, width)
        gk = acck[...] * scale
        masked = jnp.where(flags, gk, 0.0).astype(bf16)
        for pair in range(pairs):
            at = pair * LANES
            both = mm_tn(masked[:, at : at + LANES], kn[:, at : at + LANES]) * (1.0 / scale)
            pay_ref[pair * head : (pair + 1) * head] = accp[
                pair * head : (pair + 1) * head
            ] + jnp.where(lower, both[:head], both[head:])
        seg = (iota((lanes, LANES), 0) // ROWS == iota((lanes, LANES), 1)).astype(f32)
        pay_ref[pairs * head :] = lax.dot_general(
            accs[...],
            seg,
            (((1,), (0,)), ((), ())),
            precision=lax.Precision.HIGHEST,
            preferred_element_type=f32,
        )
        ret_ref[:, :width] = gk[:WINDOW].astype(bf16)
        ret_ref[:, width:] = accv[:WINDOW].astype(bf16)
        dk_ref[...] = gk[WINDOW:]
        dv_ref[...] = accv[WINDOW:]


def keys_kernel(dk_ref, dv_ref, back_ref, kw_ref, rot_ref, kgr_ref, vg_ref):
    rows, width = dk_ref.shape
    head = LANES // 2
    edge = rows - WINDOW
    back = back_ref[...].astype(f32)
    gk = jnp.concatenate([dk_ref[:edge], dk_ref[edge:] + back[:, :width]], axis=0)
    flags = byte_flags(word_bytes(kw_ref[...]), width)
    masked = jnp.where(flags, gk, 0.0).astype(bf16)
    zero = jnp.zeros((head, head), bf16)
    for pair in range(width // LANES):
        at = pair * LANES
        turn = jnp.concatenate(
            [
                jnp.concatenate([rot_ref[2 * pair].astype(bf16), zero], axis=1),
                jnp.concatenate([zero, rot_ref[2 * pair + 1].astype(bf16)], axis=1),
            ],
            axis=0,
        )
        kgr_ref[:, at : at + LANES] = mm_nt(masked[:, at : at + LANES], turn).astype(bf16)
    vg_ref[:edge] = dv_ref[:edge].astype(bf16)
    vg_ref[edge:] = (dv_ref[edge:] + back[:, width:]).astype(bf16)


def raw_kernel(groups, pay_ref, rot_ref, raw_ref, sq_ref):
    head = LANES // 2
    total = jnp.zeros((1, head), f32)
    for g in range(groups):
        part = pay_ref[(g // 2) * head : (g // 2 + 1) * head, :]
        part = part[:, (g % 2) * head : (g % 2 + 1) * head]
        raw = lax.dot_general(
            rot_ref[g],
            part,
            (((1,), (1,)), ((), ())),
            precision=lax.Precision.HIGHEST,
            preferred_element_type=f32,
        )
        raw_ref[g] = raw
        total = total + jnp.sum(raw * raw, axis=0, keepdims=True)
    sq_ref[...] = jnp.broadcast_to(jnp.sum(total, axis=1, keepdims=True), sq_ref.shape)


def all_sum(x, axis):
    size = lax.axis_size(axis)
    if size & (size - 1):
        return lax.psum(x, axis)
    step = 1
    while step < size:
        x = x + lax.ppermute(x, axis, [(i, i ^ step) for i in range(size)])
        step *= 2
    return x


def whole(shape):
    return pl.BlockSpec(shape, lambda *_: (0,) * len(shape))


def per_device(
    query_elements,
    query_exponents,
    key_elements,
    key_exponents,
    value_elements,
    value_exponents,
    query_clip_words,
    key_clip_words,
    sinks,
    rotation,
    output_gradient,
):
    rows, query_width = query_elements.shape
    groups, head, _ = rotation.shape
    per_group = sinks.shape[0] // groups
    real_width = groups * head
    padded = groups + groups % 2
    width = padded * head
    rot = rotation
    if padded != groups:
        spare = width - real_width

        def pad(x, unit):
            return jnp.pad(x, ((0, 0), (0, spare // unit)))

        key_elements, value_elements = pad(key_elements, 1), pad(value_elements, 1)
        key_exponents = pad(key_exponents, SHARED_EXPONENT)
        value_exponents = pad(value_exponents, SHARED_EXPONENT)
        key_clip_words = pad(key_clip_words, WORD_BITS)
        rot = jnp.pad(rotation, ((0, padded - groups), (0, 0), (0, 0)))
    pairs = width // LANES
    lanes = per_group // 2 * ROWS
    blocks = width // SHARED_EXPONENT
    words = width // WORD_BITS
    all_tokens = rows * lax.axis_size("seq")
    all_heads = sinks.shape[0] * lax.axis_size("head")
    limit_value = limit_factor * math.sqrt(all_tokens * all_heads * head)
    devices = range(lax.axis_size("seq"))
    forward = [(i - 1, i) for i in devices if i]
    backward = [(i, i - 1) for i in devices if i]

    tail = rows // WINDOW - 1
    halo = pl.pallas_call(
        halo_kernel,
        grid=(1,),
        in_specs=[
            pl.BlockSpec((WINDOW, n), lambda i: (tail, 0))
            for n in (width, blocks, width, blocks, words)
        ],
        out_specs=whole((WINDOW, 2 * width + LANES)),
        out_shape=jax.ShapeDtypeStruct((WINDOW, 2 * width + LANES), bf16),
        name="halo",
    )(key_elements, key_exponents, value_elements, value_exponents, key_clip_words)
    halo = lax.ppermute(halo, "seq", forward)

    def by_block(n):
        return pl.BlockSpec((ROWS, n), lambda b: (b, 0))

    pay_rows = pairs * head + 2 * padded
    grad_q, pay, back, grad_k, grad_v = pl.pallas_call(
        functools.partial(main_kernel, groups, per_group),
        grid=(rows // ROWS,),
        in_specs=[
            pl.BlockSpec(memory_space=pltpu.SMEM),
            by_block(query_width),
            by_block(query_width // SHARED_EXPONENT),
            by_block(query_width),
            by_block(query_width // WORD_BITS),
            whole((rows, width)),
            whole((rows, blocks)),
            whole((rows, width)),
            whole((rows, blocks)),
            whole((rows, words)),
            whole((WINDOW, 2 * width + LANES)),
            whole(rot.shape),
        ],
        out_specs=[
            by_block(query_width),
            whole((pay_rows, LANES)),
            whole((WINDOW, 2 * width)),
            whole((rows, width)),
            whole((rows, width)),
        ],
        out_shape=[
            jax.ShapeDtypeStruct((rows, query_width), bf16),
            jax.ShapeDtypeStruct((pay_rows, LANES), f32),
            jax.ShapeDtypeStruct((WINDOW, 2 * width), bf16),
            jax.ShapeDtypeStruct((rows, width), f32),
            jax.ShapeDtypeStruct((rows, width), f32),
        ],
        scratch_shapes=[
            pltpu.VMEM((rows + WINDOW, width), bf16),
            pltpu.VMEM((groups, rows + WINDOW, LANES), bf16),
            pltpu.VMEM((groups, rows + WINDOW, LANES), bf16),
            pltpu.VMEM((rows + WINDOW, width), f32),
            pltpu.VMEM((rows + WINDOW, width), f32),
            pltpu.VMEM((pairs * head, LANES), f32),
            pltpu.VMEM((2 * padded, lanes), f32),
            pltpu.VMEM((2 * padded, lanes), f32),
            pltpu.VMEM((ROWS, lanes), bf16),
        ],
        compiler_params=pltpu.CompilerParams(vmem_limit_bytes=48 * 1024 * 1024),
        name="attend",
    )(
        sinks,
        query_elements,
        query_exponents,
        output_gradient,
        query_clip_words,
        key_elements,
        key_exponents,
        value_elements,
        value_exponents,
        key_clip_words,
        halo,
        rot,
    )
    pay = all_sum(pay, "seq")
    back = lax.ppermute(back, "seq", backward)
    key_gradient_raw, value_gradient = pl.pallas_call(
        keys_kernel,
        out_shape=[
            jax.ShapeDtypeStruct((rows, width), bf16),
            jax.ShapeDtypeStruct((rows, width), bf16),
        ],
        name="keys",
    )(grad_k, grad_v, back, key_clip_words, rot)
    raw, square = pl.pallas_call(
        functools.partial(raw_kernel, groups),
        out_shape=[
            jax.ShapeDtypeStruct((groups, head, head), f32),
            jax.ShapeDtypeStruct((8, LANES), f32),
        ],
        name="raw",
    )(pay, rotation)
    square = all_sum(square, "head")[0, 0]
    grad_rotation = raw * (clip_scale / jnp.maximum(jnp.sqrt(square), limit_value))
    sink_sum = pay[pairs * head : pairs * head + 2 * groups, : per_group // 2]
    sink_sum = sink_sum.reshape(groups, 2, per_group // 2).transpose(0, 2, 1).reshape(-1)
    return (
        grad_q,
        key_gradient_raw[:, :real_width],
        value_gradient[:, :real_width],
        grad_rotation,
        sink_sum,
    )


def solution(mesh):
    return jax.shard_map(
        per_device,
        mesh=mesh,
        in_specs=(
            P("seq", "head"),
            P("seq", "head"),
            P("seq", "head"),
            P("seq", "head"),
            P("seq", "head"),
            P("seq", "head"),
            P("seq", "head"),
            P("seq", "head"),
            P("head"),
            P("head", None, None),
            P("seq", "head"),
        ),
        out_specs=(
            P("seq", "head"),
            P("seq", "head"),
            P("seq", "head"),
            P("head", None, None),
            P("head"),
        ),
        check_vma=False,
    )
```

```python
import functools
import math

import jax
import jax.numpy as jnp
from jax import lax
from jax.experimental import pallas as pl
from jax.experimental.pallas import tpu as pltpu
from jax.sharding import PartitionSpec as P

WINDOW = 128
SHARED_EXPONENT = 32
WORD_BITS = 16
LANES = 128
UNIT = 32
STEP = 128
BAND = WINDOW + UNIT
AHEAD = 2
LAG = 3

clip_scale = 64.0
limit_factor = 0.05
negative = -1e30

f32 = jnp.float32
bf16 = jnp.bfloat16
i32 = jnp.int32


def iota(shape, dim):
    return lax.broadcasted_iota(i32, shape, dim)


def mm(a, b):
    return lax.dot_general(a, b, (((1,), (0,)), ((), ())), preferred_element_type=f32)


def mm_nt(a, b):
    return lax.dot_general(a, b, (((1,), (1,)), ((), ())), preferred_element_type=f32)


def mm_tn(a, b):
    return lax.dot_general(a, b, (((0,), (0,)), ((), ())), preferred_element_type=f32)


def zero_one(mask):
    return mask.astype(f32).astype(bf16)


def decoded(elements, powers):
    shape = (powers.shape[0], elements.shape[1])
    spread = zero_one(iota(shape, 1) // SHARED_EXPONENT == iota(shape, 0))
    scale = mm_tn(jnp.exp2(powers.astype(f32)).astype(bf16), spread)
    return elements * scale.astype(bf16)


def word_bytes(words):
    count = words.shape[0]
    shape = (count, LANES)
    low = zero_one(iota(shape, 1) == iota(shape, 0))
    high = zero_one(iota(shape, 1) == iota(shape, 0) + count)
    first = (words & 255).astype(f32).astype(bf16)
    second = ((words >> 8) & 255).astype(f32).astype(bf16)
    return (mm_tn(first, low) + mm_tn(second, high)).astype(bf16)


def byte_flags(byte_rows, width):
    count = width // WORD_BITS
    shape = (LANES, width)
    lane, row = iota(shape, 1), iota(shape, 0)
    upper = (lane % WORD_BITS) // 8
    spread = zero_one(row == lane // WORD_BITS + upper * count)
    value = mm(byte_rows, spread).astype(i32)
    bit = jnp.left_shift(jnp.ones((1, width), i32), iota((1, width), 1) % 8)
    return (value & bit) != 0


def turn_pair(rot_ref, pair):
    first = rot_ref[2 * pair].astype(bf16)
    zero = jnp.zeros_like(first)
    second = rot_ref[2 * pair + 1].astype(bf16)
    return jnp.concatenate(
        [jnp.concatenate([first, zero], axis=1), jnp.concatenate([zero, second], axis=1)], axis=0
    )


def halo_kernel(k_ref, ke_ref, v_ref, ve_ref, w_ref, out_ref):
    width = k_ref.shape[1]
    out_ref[:, :width] = decoded(k_ref[...], ke_ref[...])
    out_ref[:, width : 2 * width] = decoded(v_ref[...], ve_ref[...])
    out_ref[:, 2 * width :] = word_bytes(w_ref[...])


def attend_step(groups, per_group, edge, refs, scratch):
    sink_ref, q_ref, qe_ref, do_ref, qw_ref, rot_ref, gq_ref = refs
    kn, kg, vg, acck, accv, accp, accs, sinks = scratch
    b = pl.program_id(0)
    side = per_group // 2
    half_lanes = side * UNIT
    lanes = 2 * half_lanes
    head = LANES // 2
    start = pl.multiple_of(b * STEP, STEP)
    words = jnp.transpose(qw_ref[...])
    scales = jnp.exp2(qe_ref[...].astype(f32))
    column = iota((UNIT, lanes), 1) % UNIT
    current = iota((UNIT, lanes), 0) <= column
    low = zero_one(iota((UNIT, lanes), 0) > column)
    lower = iota((1, LANES), 1) < head
    bit = jnp.left_shift(jnp.ones((head, 1), i32), iota((head, 1), 0) % WORD_BITS)
    per_pair = 2 * head // WORD_BITS
    per_scale = 2 * head // SHARED_EXPONENT
    shared = {}

    def turned_tile(ref, g, s):
        rows = [
            ref[s * UNIT : (s + 1) * UNIT, (side * g + p) * LANES : (side * g + p + 1) * LANES]
            for p in range(side)
        ]
        both = jnp.transpose(jnp.concatenate(rows, axis=0))
        return jnp.concatenate([both[:head], both[head:]], axis=1)

    def side_by_side(x, base, count, s):
        return jnp.concatenate(
            [
                x[base + p * count : base + (p + 1) * count, s * UNIT : (s + 1) * UNIT]
                for p in range(side)
            ],
            axis=1,
        )

    def operands(g, s):
        if (g, s) not in shared:
            scale = side_by_side(scales, g * side * per_scale, per_scale, s)
            each = per_scale // 2
            scale = jnp.concatenate(
                [
                    jnp.concatenate(
                        [
                            jnp.broadcast_to(
                                scale[odd * each + n : odd * each + n + 1],
                                (SHARED_EXPONENT, half_lanes),
                            )
                            for n in range(each)
                        ],
                        axis=0,
                    )
                    for odd in range(2)
                ],
                axis=1,
            )
            qt = turned_tile(q_ref, g, s) * scale.astype(bf16)
            shared[g, s] = (qt, turned_tile(do_ref, g, s))
        return shared[g, s]

    def pair_operands(g, s):
        other = g + 1 if g % 2 == 0 else g - 1
        mine = operands(g, s)
        theirs = operands(other, s) if other < groups else mine
        first, second = (mine, theirs) if g % 2 == 0 else (theirs, mine)
        return [jnp.concatenate([x, y], axis=0) for x, y in zip(first, second)]

    def band(s):
        return pl.ds(start + s * UNIT, BAND)

    def combined(x):
        mid = x[UNIT:WINDOW]
        return jnp.concatenate([jnp.where(current, x[WINDOW:], x[:UNIT]), mid], axis=0)

    def spread(x):
        first = x[:UNIT] * low
        return jnp.concatenate([first, x[UNIT:], x[:UNIT] - first], axis=0)

    def fetch(g, s):
        operands(g, s)
        if ("k", g // 2, s) not in shared:
            at = (g // 2) * LANES
            shared["k", g // 2, s] = jnp.transpose(kn[band(s), at : at + LANES])
        spots = side_by_side(words, g * side * per_pair, per_pair, s)
        return kg[g, band(s), :], vg[g, band(s), :], sinks[pl.ds(g, 1), :], spots

    def products(g, s, loaded):
        keys, values, _, _ = loaded
        qt, dt = operands(g, s)
        scores = mm(keys, qt)
        if edge:
            limit = jnp.where(lax.axis_index("seq") == 0, WINDOW, 0) - (start + s * UNIT)
            scores = jnp.where(iota((BAND, 1), 0) >= limit, scores, negative)
        return combined(scores), combined(mm(values, dt))

    def soft(g, s, loaded, scores, gprobs):
        sink = loaded[2]
        row_max = jnp.maximum(jnp.max(scores, axis=0, keepdims=True), sink)
        numer = jnp.exp(scores - row_max)
        sink_numer = jnp.exp(sink - row_max)
        inverse = 1.0 / (jnp.sum(numer, axis=0, keepdims=True) + sink_numer)
        weights = numer * inverse
        delta = jnp.sum(weights * gprobs, axis=0, keepdims=True)
        gscores = (weights * (gprobs - delta)).astype(bf16)
        term = sink_numer * inverse * delta
        return spread(weights.astype(bf16)), spread(gscores), term

    def gradients(g, s, probs, grads):
        ktr = shared["k", g // 2, s][(g % 2) * head : (g % 2 + 1) * head]
        both_q, both_d = pair_operands(g, s)
        return mm(ktr, grads), mm_nt(grads, both_q), mm_nt(probs, both_d)

    def clipped(g, s, loaded, dq):
        spots = loaded[3]
        each = per_pair // 2
        spots = jnp.concatenate(
            [
                jnp.concatenate(
                    [
                        jnp.broadcast_to(
                            spots[odd * each + n : odd * each + n + 1], (WORD_BITS, half_lanes)
                        )
                        for n in range(each)
                    ],
                    axis=0,
                )
                for odd in range(2)
            ],
            axis=1,
        )
        masked = jnp.where((spots & bit) != 0, dq, 0.0).astype(bf16)
        turned = mm(rot_ref[g].astype(bf16), masked).astype(bf16)
        turned = jnp.concatenate([turned[:, :half_lanes], turned[:, half_lanes:]], axis=0)
        return mm_nt(masked, pair_operands(g, s)[0]), turned

    sums = {}

    def finish(g, s, term, turned, *parts):
        turned = jnp.transpose(turned)
        for p in range(side):
            cols = (side * g + p) * LANES
            gq_ref[s * UNIT : (s + 1) * UNIT, cols : cols + LANES] = turned[
                p * UNIT : (p + 1) * UNIT
            ]
        accs[pl.ds(g, 1), :] -= term
        sums[g, s] = parts
        if g % 2 == 0 and g + 1 < groups:
            return
        pair = g // 2
        at = pair * LANES
        left = sums[2 * pair, s]
        right = parts if g % 2 else (0.0, 0.0, 0.0)
        acck[band(s), at : at + LANES] += jnp.where(lower, left[0], right[0])
        accv[band(s), at : at + LANES] += jnp.where(lower, left[1], right[1])
        accp[pair * head : (pair + 1) * head] += jnp.where(lower, left[2], right[2])

    units = [
        (g, s)
        for pair in range((groups + 1) // 2)
        for s in range(STEP // UNIT)
        for g in (2 * pair, 2 * pair + 1)
        if g < groups
    ]
    loaded, ready, rounded, part, done = {}, {}, {}, {}, {}

    def stage(n, lead):
        n += lead
        return n if 0 <= n < len(units) else None

    for turn in range(-AHEAD, len(units) + LAG):
        if (n := stage(turn, AHEAD)) is not None:
            loaded[n] = fetch(*units[n])
        if (n := stage(turn, 1)) is not None:
            ready[n] = products(*units[n], loaded[n])
        if (n := stage(turn, 0)) is not None:
            rounded[n] = soft(*units[n], loaded[n], *ready.pop(n))
        if (n := stage(turn, -1)) is not None:
            part[n] = gradients(*units[n], *rounded[n][:2])
        if (n := stage(turn, -2)) is not None:
            dq, dk, dv = part.pop(n)
            dp, turned = clipped(*units[n], loaded[n], dq)
            done[n] = (rounded[n][2], turned, dk, dv, dp)
        if (n := stage(turn, -LAG)) is not None:
            finish(*units[n], *done.pop(n))


def prepare(groups, per_group, sink_ref, keys, values, scratch):
    kn, kg, vg, _, _, _, accs, sinks = scratch
    head = LANES // 2
    side = per_group // 2
    eighth = jnp.asarray(head**-0.5, bf16)
    for at, k, v in zip((0, WINDOW), keys, values):
        k = k * eighth
        kn[at : at + k.shape[0]] = k
        for g in range(groups):
            kg[g, at : at + k.shape[0]] = k[:, g * head : (g + 1) * head]
            vg[g, at : at + k.shape[0]] = v[:, g * head : (g + 1) * head]
    lanes = per_group * UNIT
    block = iota((1, lanes), 1) // UNIT
    for g in range(groups):
        row = jnp.zeros((1, lanes), f32)
        for n in range(per_group):
            h = 2 * (n % side) + n // side
            row = jnp.where(block == n, sink_ref[g * per_group + h], row)
        sinks[pl.ds(g, 1), :] = row
    accs[...] = jnp.zeros_like(accs)


def sink_sums(groups, per_group, accs):
    side = per_group // 2
    shape = (accs.shape[0], LANES)
    row, lane = iota(shape, 0), iota(shape, 1)
    total = jnp.zeros(shape, f32)
    for n in range(per_group):
        part = jnp.sum(accs[:, n * UNIT : (n + 1) * UNIT], axis=1, keepdims=True)
        h = 2 * (n % side) + n // side
        total = total + jnp.where((lane == row * per_group + h) & (row < groups), part, 0.0)
    return jnp.sum(total, axis=0, keepdims=True)


def key_terms(gk, flags, kn_rows, pair):
    at = pair * LANES
    head = LANES // 2
    masked = jnp.where(flags[:, at : at + LANES], gk[:, at : at + LANES], 0.0).astype(bf16)
    both = mm_tn(masked, kn_rows[:, at : at + LANES]) * float(head) ** 0.5
    lower = iota((1, LANES), 1) < head
    return masked, jnp.where(lower, both[:head], both[head:])


def main_kernel(
    groups,
    per_group,
    sink_ref,
    q_ref,
    qe_ref,
    do_ref,
    qw_ref,
    k_ref,
    ke_ref,
    v_ref,
    ve_ref,
    kw_ref,
    rot_ref,
    gq_ref,
    kgr_ref,
    vgr_ref,
    front_ref,
    tail_ref,
    pay_ref,
    *scratch,
):
    kn, _, _, acck, accv, accp, accs, _ = scratch
    b = pl.program_id(0)
    rows, width = k_ref.shape
    head = LANES // 2

    @pl.when(b == 0)
    def _():
        keys = decoded(k_ref[...], ke_ref[...])
        values = decoded(v_ref[...], ve_ref[...])
        prepare(groups, per_group, sink_ref, (keys,), (values,), scratch)
        acck[...] = jnp.zeros_like(acck)
        accv[...] = jnp.zeros_like(accv)
        accp[...] = jnp.zeros_like(accp)

    refs = (sink_ref, q_ref, qe_ref, do_ref, qw_ref, rot_ref, gq_ref)
    attend_step(groups, per_group, False, refs, scratch)

    @pl.when(b == pl.num_programs(0) - 1)
    def _():
        scale = head**-0.5
        front_ref[:, :width] = acck[:WINDOW]
        front_ref[:, width:] = accv[:WINDOW]
        gk = acck[WINDOW:] * scale
        gv = accv[WINDOW:]
        tail_ref[:, :width] = gk[rows - 2 * WINDOW :]
        tail_ref[:, width:] = gv[rows - 2 * WINDOW :]
        vgr_ref[WINDOW:] = gv.astype(bf16)
        flags = byte_flags(word_bytes(kw_ref[...])[WINDOW:], width)
        for pair in range(width // LANES):
            at = pair * LANES
            masked, term = key_terms(gk, flags, kn[WINDOW:], pair)
            kgr_ref[WINDOW:, at : at + LANES] = mm_nt(masked, turn_pair(rot_ref, pair)).astype(bf16)
            pay_ref[pair * head : (pair + 1) * head] = (
                accp[pair * head : (pair + 1) * head] + term
            )
        pay_ref[width // 2 :] = jnp.broadcast_to(sink_sums(groups, per_group, accs), (8, LANES))


def front_kernel(
    groups,
    per_group,
    sink_ref,
    q_ref,
    qe_ref,
    do_ref,
    qw_ref,
    k_ref,
    ke_ref,
    v_ref,
    ve_ref,
    kw_ref,
    rot_ref,
    halo_ref,
    front_ref,
    part_ref,
    gq_in,
    kgr_in,
    vgr_in,
    gq_ref,
    kgr_ref,
    vgr_ref,
    ret_ref,
    pay_ref,
    *scratch,
):
    kn, _, _, acck, accv, accp, accs, _ = scratch
    b = pl.program_id(0)
    width = k_ref.shape[1]
    head = LANES // 2

    @pl.when(b == 0)
    def _():
        keys = decoded(k_ref[...], ke_ref[...])
        values = decoded(v_ref[...], ve_ref[...])
        keys = (halo_ref[:, :width], keys)
        values = (halo_ref[:, width : 2 * width], values)
        prepare(groups, per_group, sink_ref, keys, values, scratch)
        acck[:WINDOW] = jnp.zeros((WINDOW, width), f32)
        accv[:WINDOW] = jnp.zeros((WINDOW, width), f32)
        acck[WINDOW:] = front_ref[:, :width]
        accv[WINDOW:] = front_ref[:, width:]
        accp[...] = part_ref[: width // 2]

    refs = (sink_ref, q_ref, qe_ref, do_ref, qw_ref, rot_ref, gq_ref)
    attend_step(groups, per_group, True, refs, scratch)

    @pl.when(b == pl.num_programs(0) - 1)
    def _():
        gk = acck[...] * (head**-0.5)
        ret_ref[:, :width] = gk[:WINDOW].astype(bf16)
        ret_ref[:, width:] = accv[:WINDOW].astype(bf16)
        vgr_ref[...] = accv[WINDOW:].astype(bf16)
        bytes_all = jnp.concatenate([halo_ref[:, 2 * width :], word_bytes(kw_ref[...])], axis=0)
        flags = byte_flags(bytes_all, width)
        for pair in range(width // LANES):
            at = pair * LANES
            masked, term = key_terms(gk, flags, kn[...], pair)
            kgr_ref[:, at : at + LANES] = mm_nt(
                masked[WINDOW:], turn_pair(rot_ref, pair)
            ).astype(bf16)
            pay_ref[pair * head : (pair + 1) * head] = (
                accp[pair * head : (pair + 1) * head] + term
            )
        pay_ref[width // 2 :] = part_ref[width // 2 :] + sink_sums(groups, per_group, accs)


def keys_kernel(tail_ref, back_ref, kw_ref, rot_ref, kgr_in, vgr_in, kgr_ref, vgr_ref):
    width = kgr_ref.shape[1]
    both = tail_ref[...] + back_ref[...].astype(f32)
    flags = byte_flags(word_bytes(kw_ref[...]), width)
    masked = jnp.where(flags, both[:, :width], 0.0).astype(bf16)
    for pair in range(width // LANES):
        at = pair * LANES
        kgr_ref[:, at : at + LANES] = mm_nt(
            masked[:, at : at + LANES], turn_pair(rot_ref, pair)
        ).astype(bf16)
    vgr_ref[...] = both[:, width:].astype(bf16)


def raw_kernel(groups, rot_ref, *refs):
    *pays, raw_ref, sq_ref, sink_ref = refs
    head = LANES // 2
    pay = pays[0][...]
    for x in pays[1:]:
        pay = pay + x[...]
    total = jnp.zeros((1, head), f32)
    for g in range(groups):
        part = pay[(g // 2) * head : (g // 2 + 1) * head, (g % 2) * head : (g % 2 + 1) * head]
        raw = lax.dot_general(
            rot_ref[g],
            part,
            (((1,), (1,)), ((), ())),
            precision=lax.Precision.HIGHEST,
            preferred_element_type=f32,
        )
        raw_ref[g] = raw
        total = total + jnp.sum(raw * raw, axis=0, keepdims=True)
    sq_ref[...] = jnp.broadcast_to(jnp.sum(total, axis=1, keepdims=True), sq_ref.shape)
    sink_ref[...] = pay[pay.shape[0] - 8 : pay.shape[0] - 7, : sink_ref.shape[1]]


def scale_kernel(limit_value, raw_ref, *refs):
    *squares, out_ref = refs
    square = squares[0][:1, :1]
    for x in squares[1:]:
        square = square + x[:1, :1]
    factor = clip_scale / jnp.maximum(jnp.sqrt(square), limit_value)
    for g in range(raw_ref.shape[0]):
        out_ref[g] = raw_ref[g] * factor


def addends(x, axis):
    size = lax.axis_size(axis)
    if size & (size - 1):
        return [lax.psum(x, axis)]
    step, parts = 1, [x]
    while step < size:
        x = functools.reduce(jnp.add, parts)
        masks = (step, 2 * step, 3 * step) if 2 * step < size else (step,)
        swaps = [[(i, i ^ m) for i in range(size)] for m in masks]
        parts = [x] + [lax.ppermute(x, axis, swap) for swap in swaps]
        step *= 4
    return parts


def whole(shape):
    return pl.BlockSpec(shape, lambda *_: (0,) * len(shape))


def per_device(
    query_elements,
    query_exponents,
    key_elements,
    key_exponents,
    value_elements,
    value_exponents,
    query_clip_words,
    key_clip_words,
    sinks,
    rotation,
    output_gradient,
):
    rows, query_width = query_elements.shape
    groups, head, _ = rotation.shape
    per_group = sinks.shape[0] // groups
    real_width = groups * head
    padded = groups + groups % 2
    width = padded * head
    rot = rotation
    key_powers, value_powers = key_exponents.T, value_exponents.T
    key_words = key_clip_words.T
    if padded != groups:
        spare = width - real_width
        key_elements = jnp.pad(key_elements, ((0, 0), (0, spare)))
        value_elements = jnp.pad(value_elements, ((0, 0), (0, spare)))
        key_powers = jnp.pad(key_powers, ((0, spare // SHARED_EXPONENT), (0, 0)))
        value_powers = jnp.pad(value_powers, ((0, spare // SHARED_EXPONENT), (0, 0)))
        key_words = jnp.pad(key_words, ((0, spare // WORD_BITS), (0, 0)))
        rot = jnp.pad(rotation, ((0, padded - groups), (0, 0), (0, 0)))
    lanes = per_group * UNIT
    blocks = width // SHARED_EXPONENT
    words = width // WORD_BITS
    all_tokens = rows * lax.axis_size("seq")
    all_heads = sinks.shape[0] * lax.axis_size("head")
    limit_value = limit_factor * math.sqrt(all_tokens * all_heads * head)
    devices = range(lax.axis_size("seq"))
    forward = [(i - 1, i) for i in devices if i]
    backward = [(i, i - 1) for i in devices if i]
    key_args = (key_elements, key_powers, value_elements, value_powers, key_words)

    def key_specs(count, index):
        return [
            pl.BlockSpec((count, width), lambda *_: (index, 0)),
            pl.BlockSpec((blocks, count), lambda *_: (0, index)),
            pl.BlockSpec((count, width), lambda *_: (index, 0)),
            pl.BlockSpec((blocks, count), lambda *_: (0, index)),
            pl.BlockSpec((words, count), lambda *_: (0, index)),
        ]

    last = rows // WINDOW - 1
    halo = pl.pallas_call(
        halo_kernel,
        grid=(1,),
        in_specs=key_specs(WINDOW, last),
        out_specs=whole((WINDOW, 2 * width + LANES)),
        out_shape=jax.ShapeDtypeStruct((WINDOW, 2 * width + LANES), bf16),
        name="halo",
    )(*key_args)
    halo = lax.ppermute(halo, "seq", forward)

    skip = WINDOW // STEP
    pay_rows = width // 2 + 8
    query_args = (sinks, query_elements, query_exponents.T, output_gradient, query_clip_words)

    def query_specs(offset):
        def rows_of(n):
            return pl.BlockSpec((STEP, n), lambda b: (b + offset, 0))

        powers = query_width // SHARED_EXPONENT
        return [
            pl.BlockSpec(memory_space=pltpu.SMEM),
            rows_of(query_width),
            pl.BlockSpec((powers, STEP), lambda b: (0, b + offset)),
            rows_of(query_width),
            rows_of(query_width // WORD_BITS),
        ]

    def scratch(count):
        return [
            pltpu.VMEM((count, width), bf16),
            pltpu.VMEM((groups, count, head), bf16),
            pltpu.VMEM((groups, count, head), bf16),
            pltpu.VMEM((count, width), f32),
            pltpu.VMEM((count, width), f32),
            pltpu.VMEM((width // 2, LANES), f32),
            pltpu.VMEM((8, lanes), f32),
            pltpu.VMEM((8, lanes), f32),
        ]

    params = pltpu.CompilerParams(vmem_limit_bytes=40 * 1024 * 1024)
    full_q = jax.ShapeDtypeStruct((rows, query_width), bf16)
    full_k = jax.ShapeDtypeStruct((rows, width), bf16)
    edge_f = jax.ShapeDtypeStruct((WINDOW, 2 * width), f32)
    pay_f = jax.ShapeDtypeStruct((pay_rows, LANES), f32)
    grad_q, kgr, vgr, front, tail, part = pl.pallas_call(
        functools.partial(main_kernel, groups, per_group),
        grid=(rows // STEP - skip,),
        in_specs=query_specs(skip) + key_specs(rows, 0) + [whole(rot.shape)],
        out_specs=[
            pl.BlockSpec((STEP, query_width), lambda b: (b + skip, 0)),
            whole((rows, width)),
            whole((rows, width)),
            whole((WINDOW, 2 * width)),
            whole((WINDOW, 2 * width)),
            whole((pay_rows, LANES)),
        ],
        out_shape=[full_q, full_k, full_k, edge_f, edge_f, pay_f],
        scratch_shapes=scratch(rows),
        compiler_params=params,
        cost_estimate=pl.CostEstimate(
            flops=60_000_000_000, bytes_accessed=60_000_000, transcendentals=0
        ),
        name="attend",
    )(*query_args, *key_args, rot)

    anywhere = pl.BlockSpec(memory_space=pl.ANY)
    grad_q, kgr, vgr, back, pay = pl.pallas_call(
        functools.partial(front_kernel, groups, per_group),
        grid=(skip,),
        in_specs=query_specs(0)
        + key_specs(WINDOW, 0)
        + [
            whole(rot.shape),
            whole((WINDOW, 2 * width + LANES)),
            whole((WINDOW, 2 * width)),
            whole((pay_rows, LANES)),
            anywhere,
            anywhere,
            anywhere,
        ],
        out_specs=[
            pl.BlockSpec((STEP, query_width), lambda b: (b, 0)),
            whole((WINDOW, width)),
            whole((WINDOW, width)),
            whole((WINDOW, 2 * width)),
            whole((pay_rows, LANES)),
        ],
        out_shape=[
            full_q,
            full_k,
            full_k,
            jax.ShapeDtypeStruct((WINDOW, 2 * width), bf16),
            pay_f,
        ],
        input_output_aliases={14: 0, 15: 1, 16: 2},
        scratch_shapes=scratch(2 * WINDOW),
        compiler_params=params,
        name="front",
    )(*query_args, *key_args, rot, halo, front, part, grad_q, kgr, vgr)

    pays = addends(pay, "seq")
    back = lax.ppermute(back, "seq", backward)
    kgr, vgr = pl.pallas_call(
        keys_kernel,
        grid=(1,),
        in_specs=[
            whole((WINDOW, 2 * width)),
            whole((WINDOW, 2 * width)),
            pl.BlockSpec((words, WINDOW), lambda b: (0, last)),
            whole(rot.shape),
            anywhere,
            anywhere,
        ],
        out_specs=[pl.BlockSpec((WINDOW, width), lambda b: (last, 0))] * 2,
        out_shape=[full_k, full_k],
        input_output_aliases={4: 0, 5: 1},
        cost_estimate=pl.CostEstimate(
            flops=1_000_000_000, bytes_accessed=3_000_000, transcendentals=0
        ),
        name="keys",
    )(tail, back, key_words, rot, kgr, vgr)
    raw, square, sink_sum = pl.pallas_call(
        functools.partial(raw_kernel, groups),
        out_shape=[
            jax.ShapeDtypeStruct((groups, head, head), f32),
            jax.ShapeDtypeStruct((8, LANES), f32),
            jax.ShapeDtypeStruct((1, sinks.shape[0]), f32),
        ],
        name="raw",
    )(rotation, *pays)
    grad_rotation = pl.pallas_call(
        functools.partial(scale_kernel, limit_value),
        out_shape=jax.ShapeDtypeStruct((groups, head, head), f32),
        name="scale",
    )(raw, *addends(square, "head"))
    return (
        grad_q,
        kgr[:, :real_width],
        vgr[:, :real_width],
        grad_rotation,
        sink_sum.reshape(-1),
    )


def solution(mesh):
    return jax.shard_map(
        per_device,
        mesh=mesh,
        in_specs=(
            P("seq", "head"),
            P("seq", "head"),
            P("seq", "head"),
            P("seq", "head"),
            P("seq", "head"),
            P("seq", "head"),
            P("seq", "head"),
            P("seq", "head"),
            P("head"),
            P("head", None, None),
            P("seq", "head"),
        ),
        out_specs=(
            P("seq", "head"),
            P("seq", "head"),
            P("seq", "head"),
            P("head", None, None),
            P("head"),
        ),
        check_vma=False,
    )
```

```python
import functools
import math

import jax
import jax.numpy as jnp
from jax import lax
from jax.experimental import pallas as pl
from jax.experimental.pallas import tpu as pltpu
from jax.sharding import PartitionSpec as P


WINDOW = 128
SHARED_EXPONENT = 32
WORD_BITS = 16
LANES = 128
UNIT = 32
STEP = 128
BAND = WINDOW + UNIT
AHEAD = 2
LAG = 3

clip_scale = 64.0
limit_factor = 0.05
negative = -1e30

f32 = jnp.float32
bf16 = jnp.bfloat16
i32 = jnp.int32


def iota(shape, dim):
    return lax.broadcasted_iota(i32, shape, dim)


def mm(a, b):
    return lax.dot_general(a, b, (((1,), (0,)), ((), ())), preferred_element_type=f32)


def mm_nt(a, b):
    return lax.dot_general(a, b, (((1,), (1,)), ((), ())), preferred_element_type=f32)


def mm_tn(a, b):
    return lax.dot_general(a, b, (((0,), (0,)), ((), ())), preferred_element_type=f32)


def zero_one(mask):
    return mask.astype(f32).astype(bf16)


def decoded(elements, powers):
    shape = (powers.shape[0], elements.shape[1])
    spread = zero_one(iota(shape, 1) // SHARED_EXPONENT == iota(shape, 0))
    scale = mm_tn(jnp.exp2(powers.astype(f32)).astype(bf16), spread)
    return elements * scale.astype(bf16)


def word_bytes(words):
    count = words.shape[0]
    shape = (count, LANES)
    low = zero_one(iota(shape, 1) == iota(shape, 0))
    high = zero_one(iota(shape, 1) == iota(shape, 0) + count)
    first = (words & 255).astype(f32).astype(bf16)
    second = ((words >> 8) & 255).astype(f32).astype(bf16)
    return (mm_tn(first, low) + mm_tn(second, high)).astype(bf16)


def byte_flags(byte_rows, width):
    count = width // WORD_BITS
    shape = (LANES, width)
    lane, row = iota(shape, 1), iota(shape, 0)
    upper = (lane % WORD_BITS) // 8
    spread = zero_one(row == lane // WORD_BITS + upper * count)
    value = mm(byte_rows, spread).astype(i32)
    bit = jnp.left_shift(jnp.ones((1, width), i32), iota((1, width), 1) % 8)
    return (value & bit) != 0


def turn_pair(rot_ref, pair):
    first = rot_ref[2 * pair].astype(bf16)
    zero = jnp.zeros_like(first)
    second = rot_ref[2 * pair + 1].astype(bf16)
    return jnp.concatenate(
        [jnp.concatenate([first, zero], axis=1), jnp.concatenate([zero, second], axis=1)], axis=0
    )


def halo_kernel(k_ref, ke_ref, v_ref, ve_ref, w_ref, out_ref):
    width = k_ref.shape[1]
    out_ref[:, :width] = decoded(k_ref[...], ke_ref[...])
    out_ref[:, width : 2 * width] = decoded(v_ref[...], ve_ref[...])
    out_ref[:, 2 * width :] = word_bytes(w_ref[...])


def attend_step(groups, per_group, edge, refs, scratch):
    _, q_ref, qe_ref, do_ref, qw_ref, rot_ref, gq_ref = refs
    kn, kg, vg, acck, accv, accp, accs, sinks = scratch
    b = pl.program_id(0)
    side = per_group // 2
    half_lanes = side * UNIT
    lanes = 2 * half_lanes
    head = LANES // 2
    start = pl.multiple_of(b * STEP, STEP)
    words = jnp.transpose(qw_ref[...])
    scales = jnp.exp2(qe_ref[...].astype(f32))
    column = iota((UNIT, lanes), 1) % UNIT
    current = iota((UNIT, lanes), 0) <= column
    low = zero_one(iota((UNIT, lanes), 0) > column)
    lower = iota((1, LANES), 1) < head
    bit = jnp.left_shift(jnp.ones((head, 1), i32), iota((head, 1), 0) % WORD_BITS)
    per_pair = 2 * head // WORD_BITS
    per_scale = 2 * head // SHARED_EXPONENT
    shared = {}

    def turned_tile(ref, g, s):
        rows = [
            ref[s * UNIT : (s + 1) * UNIT, (side * g + p) * LANES : (side * g + p + 1) * LANES]
            for p in range(side)
        ]
        both = jnp.transpose(jnp.concatenate(rows, axis=0))
        return jnp.concatenate([both[:head], both[head:]], axis=1)

    def side_by_side(x, base, count, s):
        return jnp.concatenate(
            [
                x[base + p * count : base + (p + 1) * count, s * UNIT : (s + 1) * UNIT]
                for p in range(side)
            ],
            axis=1,
        )

    def operands(g, s):
        if (g, s) not in shared:
            scale = side_by_side(scales, g * side * per_scale, per_scale, s)
            each = per_scale // 2
            scale = jnp.concatenate(
                [
                    jnp.concatenate(
                        [
                            jnp.broadcast_to(
                                scale[odd * each + n : odd * each + n + 1],
                                (SHARED_EXPONENT, half_lanes),
                            )
                            for n in range(each)
                        ],
                        axis=0,
                    )
                    for odd in range(2)
                ],
                axis=1,
            )
            qt = turned_tile(q_ref, g, s) * scale.astype(bf16)
            shared[g, s] = (qt, turned_tile(do_ref, g, s))
        return shared[g, s]

    def pair_operands(g, s):
        other = g + 1 if g % 2 == 0 else g - 1
        mine = operands(g, s)
        theirs = operands(other, s) if other < groups else mine
        first, second = (mine, theirs) if g % 2 == 0 else (theirs, mine)
        return [jnp.concatenate([x, y], axis=0) for x, y in zip(first, second)]

    def band(s):
        return pl.ds(start + s * UNIT, BAND)

    def combined(x):
        mid = x[UNIT:WINDOW]
        return jnp.concatenate([jnp.where(current, x[WINDOW:], x[:UNIT]), mid], axis=0)

    def spread(x):
        first = x[:UNIT] * low
        return jnp.concatenate([first, x[UNIT:], x[:UNIT] - first], axis=0)

    def fetch(g, s):
        operands(g, s)
        if ("k", g // 2, s) not in shared:
            at = (g // 2) * LANES
            shared["k", g // 2, s] = jnp.transpose(kn[band(s), at : at + LANES])
        spots = side_by_side(words, g * side * per_pair, per_pair, s)
        return kg[g, band(s), :], vg[g, band(s), :], sinks[pl.ds(g, 1), :], spots

    def products(g, s, loaded):
        keys, values, _, _ = loaded
        qt, dt = operands(g, s)
        scores = mm(keys, qt)
        if edge:
            limit = jnp.where(lax.axis_index("seq") == 0, WINDOW, 0) - (start + s * UNIT)
            scores = jnp.where(iota((BAND, 1), 0) >= limit, scores, negative)
        return combined(scores), combined(mm(values, dt))

    def soft(g, s, loaded, scores, gprobs):
        sink = loaded[2]
        row_max = jnp.maximum(jnp.max(scores, axis=0, keepdims=True), sink)
        numer = jnp.exp(scores - row_max)
        sink_numer = jnp.exp(sink - row_max)
        inverse = 1.0 / (jnp.sum(numer, axis=0, keepdims=True) + sink_numer)
        weights = numer * inverse
        delta = jnp.sum(weights * gprobs, axis=0, keepdims=True)
        gscores = (weights * (gprobs - delta)).astype(bf16)
        term = sink_numer * inverse * delta
        return spread(weights.astype(bf16)), spread(gscores), term

    def gradients(g, s, probs, grads):
        ktr = shared["k", g // 2, s][(g % 2) * head : (g % 2 + 1) * head]
        both_q, both_d = pair_operands(g, s)
        return mm(ktr, grads), mm_nt(grads, both_q), mm_nt(probs, both_d)

    def clipped(g, s, loaded, dq):
        spots = loaded[3]
        each = per_pair // 2
        spots = jnp.concatenate(
            [
                jnp.concatenate(
                    [
                        jnp.broadcast_to(
                            spots[odd * each + n : odd * each + n + 1], (WORD_BITS, half_lanes)
                        )
                        for n in range(each)
                    ],
                    axis=0,
                )
                for odd in range(2)
            ],
            axis=1,
        )
        masked = jnp.where((spots & bit) != 0, dq, 0.0).astype(bf16)
        turned = mm(rot_ref[g].astype(bf16), masked).astype(bf16)
        turned = jnp.concatenate([turned[:, :half_lanes], turned[:, half_lanes:]], axis=0)
        return mm_nt(masked, pair_operands(g, s)[0]), turned

    sums = {}

    def finish(g, s, term, turned, *parts):
        turned = jnp.transpose(turned)
        for p in range(side):
            cols = (side * g + p) * LANES
            gq_ref[s * UNIT : (s + 1) * UNIT, cols : cols + LANES] = turned[
                p * UNIT : (p + 1) * UNIT
            ]
        accs[pl.ds(g, 1), :] -= term
        sums[g, s] = parts
        if g % 2 == 0 and g + 1 < groups:
            return
        pair = g // 2
        at = pair * LANES
        left = sums[2 * pair, s]
        right = parts if g % 2 else (0.0, 0.0, 0.0)
        acck[band(s), at : at + LANES] += jnp.where(lower, left[0], right[0])
        accv[band(s), at : at + LANES] += jnp.where(lower, left[1], right[1])
        accp[pair * head : (pair + 1) * head] += jnp.where(lower, left[2], right[2])

    units = [
        (g, s)
        for pair in range((groups + 1) // 2)
        for s in range(STEP // UNIT)
        for g in (2 * pair, 2 * pair + 1)
        if g < groups
    ]
    loaded, ready, rounded, part, done = {}, {}, {}, {}, {}

    def stage(n, lead):
        n += lead
        return n if 0 <= n < len(units) else None

    for turn in range(-AHEAD, len(units) + LAG):
        if (n := stage(turn, AHEAD)) is not None:
            loaded[n] = fetch(*units[n])
        if (n := stage(turn, 1)) is not None:
            ready[n] = products(*units[n], loaded[n])
        if (n := stage(turn, 0)) is not None:
            rounded[n] = soft(*units[n], loaded[n], *ready.pop(n))
        if (n := stage(turn, -1)) is not None:
            part[n] = gradients(*units[n], *rounded[n][:2])
        if (n := stage(turn, -2)) is not None:
            dq, dk, dv = part.pop(n)
            dp, turned = clipped(*units[n], loaded[n], dq)
            done[n] = (rounded[n][2], turned, dk, dv, dp)
        if (n := stage(turn, -LAG)) is not None:
            finish(*units[n], *done.pop(n))


def prepare(groups, per_group, sink_ref, keys, values, scratch):
    kn, kg, vg, _, _, _, accs, sinks = scratch
    head = LANES // 2
    side = per_group // 2
    eighth = jnp.asarray(head**-0.5, bf16)
    for at, k, v in zip((0, WINDOW), keys, values):
        k = k * eighth
        kn[at : at + k.shape[0]] = k
        for g in range(groups):
            kg[g, at : at + k.shape[0]] = k[:, g * head : (g + 1) * head]
            vg[g, at : at + k.shape[0]] = v[:, g * head : (g + 1) * head]
    lanes = per_group * UNIT
    block = iota((1, lanes), 1) // UNIT
    for g in range(groups):
        row = jnp.zeros((1, lanes), f32)
        for n in range(per_group):
            h = 2 * (n % side) + n // side
            row = jnp.where(block == n, sink_ref[g * per_group + h], row)
        sinks[pl.ds(g, 1), :] = row
    accs[...] = jnp.zeros_like(accs)


def sink_sums(groups, per_group, accs):
    side = per_group // 2
    shape = (accs.shape[0], LANES)
    row, lane = iota(shape, 0), iota(shape, 1)
    total = jnp.zeros(shape, f32)
    for n in range(per_group):
        part = jnp.sum(accs[:, n * UNIT : (n + 1) * UNIT], axis=1, keepdims=True)
        h = 2 * (n % side) + n // side
        total = total + jnp.where((lane == row * per_group + h) & (row < groups), part, 0.0)
    return jnp.sum(total, axis=0, keepdims=True)


def key_terms(gk, flags, kn_rows, pair):
    at = pair * LANES
    head = LANES // 2
    masked = jnp.where(flags[:, at : at + LANES], gk[:, at : at + LANES], 0.0).astype(bf16)
    both = mm_tn(masked, kn_rows[:, at : at + LANES]) * float(head) ** 0.5
    lower = iota((1, LANES), 1) < head
    return masked, jnp.where(lower, both[:head], both[head:])


def main_kernel(
    groups,
    per_group,
    sink_ref,
    q_ref,
    qe_ref,
    do_ref,
    qw_ref,
    k_ref,
    ke_ref,
    v_ref,
    ve_ref,
    kw_ref,
    rot_ref,
    gq_ref,
    kgr_ref,
    vgr_ref,
    front_ref,
    tail_ref,
    pay_ref,
    *scratch,
):
    kn, _, _, acck, accv, accp, accs, _ = scratch
    b = pl.program_id(0)
    rows, width = k_ref.shape
    head = LANES // 2

    @pl.when(b == 0)
    def _():
        keys = decoded(k_ref[...], ke_ref[...])
        values = decoded(v_ref[...], ve_ref[...])
        prepare(groups, per_group, sink_ref, (keys,), (values,), scratch)
        acck[...] = jnp.zeros_like(acck)
        accv[...] = jnp.zeros_like(accv)
        accp[...] = jnp.zeros_like(accp)

    refs = (sink_ref, q_ref, qe_ref, do_ref, qw_ref, rot_ref, gq_ref)
    attend_step(groups, per_group, False, refs, scratch)

    @pl.when(b == pl.num_programs(0) - 1)
    def _():
        scale = head**-0.5
        front_ref[:, :width] = acck[:WINDOW]
        front_ref[:, width:] = accv[:WINDOW]
        gk = acck[WINDOW:] * scale
        gv = accv[WINDOW:]
        tail_ref[:, :width] = gk[rows - 2 * WINDOW :]
        tail_ref[:, width:] = gv[rows - 2 * WINDOW :]
        vgr_ref[WINDOW:] = gv.astype(bf16)
        flags = byte_flags(word_bytes(kw_ref[...])[WINDOW:], width)
        for pair in range(width // LANES):
            at = pair * LANES
            masked, term = key_terms(gk, flags, kn[WINDOW:], pair)
            kgr_ref[WINDOW:, at : at + LANES] = mm_nt(masked, turn_pair(rot_ref, pair)).astype(bf16)
            pay_ref[pair * head : (pair + 1) * head] = (
                accp[pair * head : (pair + 1) * head] + term
            )
        pay_ref[width // 2 :] = jnp.broadcast_to(sink_sums(groups, per_group, accs), (16, LANES))


def front_kernel(
    groups,
    per_group,
    sink_ref,
    q_ref,
    qe_ref,
    do_ref,
    qw_ref,
    k_ref,
    ke_ref,
    v_ref,
    ve_ref,
    kw_ref,
    rot_ref,
    halo_ref,
    front_ref,
    part_ref,
    gq_in,
    kgr_in,
    vgr_in,
    gq_ref,
    kgr_ref,
    vgr_ref,
    ret_ref,
    pay_ref,
    send_ref,
    *scratch,
):
    kn, _, _, acck, accv, accp, accs, _ = scratch
    b = pl.program_id(0)
    width = k_ref.shape[1]
    head = LANES // 2

    @pl.when(b == 0)
    def _():
        keys = decoded(k_ref[...], ke_ref[...])
        values = decoded(v_ref[...], ve_ref[...])
        keys = (halo_ref[:, :width], keys)
        values = (halo_ref[:, width : 2 * width], values)
        prepare(groups, per_group, sink_ref, keys, values, scratch)
        acck[:WINDOW] = jnp.zeros((WINDOW, width), f32)
        accv[:WINDOW] = jnp.zeros((WINDOW, width), f32)
        acck[WINDOW:] = front_ref[:, :width]
        accv[WINDOW:] = front_ref[:, width:]
        accp[...] = part_ref[: width // 2]

    refs = (sink_ref, q_ref, qe_ref, do_ref, qw_ref, rot_ref, gq_ref)
    attend_step(groups, per_group, True, refs, scratch)

    @pl.when(b == pl.num_programs(0) - 1)
    def _():
        gk = acck[...] * (head**-0.5)
        ret_ref[:, :width] = gk[:WINDOW].astype(bf16)
        ret_ref[:, width:] = accv[:WINDOW].astype(bf16)
        vgr_ref[...] = accv[WINDOW:].astype(bf16)
        bytes_all = jnp.concatenate([halo_ref[:, 2 * width :], word_bytes(kw_ref[...])], axis=0)
        flags = byte_flags(bytes_all, width)
        for pair in range(width // LANES):
            at = pair * LANES
            masked, term = key_terms(gk, flags, kn[...], pair)
            kgr_ref[:, at : at + LANES] = mm_nt(
                masked[WINDOW:], turn_pair(rot_ref, pair)
            ).astype(bf16)
            pay_ref[pair * head : (pair + 1) * head] = (
                accp[pair * head : (pair + 1) * head] + term
            )
        sink = part_ref[width // 2 : width // 2 + 1] + sink_sums(groups, per_group, accs)
        tail_row = iota((16, LANES), 0)
        pay_ref[width // 2 :] = jnp.where(tail_row == 0, sink, 0.0)
        send_ref[: width // 2] = pay_ref[: width // 2].astype(bf16)
        rest = sink - sink.astype(bf16).astype(f32)
        send_ref[width // 2 :] = jnp.where(
            tail_row == 0, sink, jnp.where(tail_row == 1, rest, 0.0)
        ).astype(bf16)


def keys_kernel(tail_ref, back_ref, kw_ref, rot_ref, kgr_in, vgr_in, kgr_ref, vgr_ref):
    width = kgr_ref.shape[1]
    both = tail_ref[...] + back_ref[...].astype(f32)
    flags = byte_flags(word_bytes(kw_ref[...]), width)
    masked = jnp.where(flags, both[:, :width], 0.0).astype(bf16)
    for pair in range(width // LANES):
        at = pair * LANES
        kgr_ref[:, at : at + LANES] = mm_nt(
            masked[:, at : at + LANES], turn_pair(rot_ref, pair)
        ).astype(bf16)
    vgr_ref[...] = both[:, width:].astype(bf16)


def raw_kernel(groups, rot_ref, *refs):
    *pays, raw_ref, sq_ref, sink_ref = refs
    head = LANES // 2
    pay = pays[0][...]
    for x in pays[1:]:
        pay = pay + x[...].astype(f32)
    total = jnp.zeros((1, head), f32)
    for g in range(groups):
        part = pay[(g // 2) * head : (g // 2 + 1) * head, (g % 2) * head : (g % 2 + 1) * head]
        raw = lax.dot_general(
            rot_ref[g],
            part,
            (((1,), (1,)), ((), ())),
            precision=lax.Precision.HIGHEST,
            preferred_element_type=f32,
        )
        raw_ref[g] = raw
        total = total + jnp.sum(raw * raw, axis=0, keepdims=True)
    sq_ref[...] = jnp.broadcast_to(jnp.sum(total, axis=1, keepdims=True), sq_ref.shape)
    at = pay.shape[0] - 16
    sink_ref[...] = (pay[at : at + 1] + pay[at + 1 : at + 2])[:, : sink_ref.shape[1]]


def scale_kernel(limit_value, raw_ref, *refs):
    *squares, out_ref = refs
    square = squares[0][:1, :1]
    for x in squares[1:]:
        square = square + x[:1, :1]
    factor = clip_scale / jnp.maximum(jnp.sqrt(square), limit_value)
    for g in range(raw_ref.shape[0]):
        out_ref[g] = raw_ref[g] * factor


def addends(x, axis, send=None, pack=None):
    size = lax.axis_size(axis)
    if size & (size - 1):
        return [lax.psum(x, axis)]
    step, parts = 1, [x]
    while step < size:
        if step > 1:
            x = functools.reduce(jnp.add, [part.astype(f32) for part in parts])
            send = None if pack is None else pack(x)
        masks = (step, 2 * step, 3 * step) if 2 * step < size else (step,)
        swaps = [[(i, i ^ m) for i in range(size)] for m in masks]
        out = x if send is None else send
        parts = [x]
        for swap in swaps:
            parts.append(lax.ppermute(out, axis, swap))
        step *= 4
    return parts


def packed(rows, x):
    rest = x - lax.reduce_precision(x, 8, 7)
    moved = jnp.concatenate([rest[-1:], rest[:-1]], axis=0)
    row = iota(x.shape, 0)
    return jnp.where(row == rows + 1, x + moved, x).astype(bf16)


def whole(shape):
    return pl.BlockSpec(shape, lambda *_: (0,) * len(shape))


def device_work(
    query_elements,
    query_exponents,
    key_elements,
    key_exponents,
    value_elements,
    value_exponents,
    query_clip_words,
    key_clip_words,
    sinks,
    rotation,
    output_gradient,
):
    rows, query_width = query_elements.shape
    groups, head, _ = rotation.shape
    per_group = sinks.shape[0] // groups
    real_width = groups * head
    padded = groups + groups % 2
    width = padded * head
    rot = rotation
    key_powers, value_powers = key_exponents.T, value_exponents.T
    key_words = key_clip_words.T
    if padded != groups:
        spare = width - real_width
        key_elements = jnp.pad(key_elements, ((0, 0), (0, spare)))
        value_elements = jnp.pad(value_elements, ((0, 0), (0, spare)))
        key_powers = jnp.pad(key_powers, ((0, spare // SHARED_EXPONENT), (0, 0)))
        value_powers = jnp.pad(value_powers, ((0, spare // SHARED_EXPONENT), (0, 0)))
        key_words = jnp.pad(key_words, ((0, spare // WORD_BITS), (0, 0)))
        rot = jnp.pad(rotation, ((0, padded - groups), (0, 0), (0, 0)))
    lanes = per_group * UNIT
    blocks = width // SHARED_EXPONENT
    words = width // WORD_BITS
    all_tokens = rows * lax.axis_size("seq")
    all_heads = sinks.shape[0] * lax.axis_size("head")
    limit_value = limit_factor * math.sqrt(all_tokens * all_heads * head)
    devices = range(lax.axis_size("seq"))
    forward = [(i - 1, i) for i in devices if i]
    backward = [(i, i - 1) for i in devices if i]
    key_args = (key_elements, key_powers, value_elements, value_powers, key_words)

    def key_specs(count, index):
        return [
            pl.BlockSpec((count, width), lambda *_: (index, 0)),
            pl.BlockSpec((blocks, count), lambda *_: (0, index)),
            pl.BlockSpec((count, width), lambda *_: (index, 0)),
            pl.BlockSpec((blocks, count), lambda *_: (0, index)),
            pl.BlockSpec((words, count), lambda *_: (0, index)),
        ]

    last = rows // WINDOW - 1
    halo = pl.pallas_call(
        halo_kernel,
        grid=(1,),
        in_specs=key_specs(WINDOW, last),
        out_specs=whole((WINDOW, 2 * width + LANES)),
        out_shape=jax.ShapeDtypeStruct((WINDOW, 2 * width + LANES), bf16),
        name="halo",
    )(*key_args)
    halo = lax.ppermute(halo, "seq", forward)

    skip = WINDOW // STEP
    pay_rows = width // 2 + 16
    query_args = (sinks, query_elements, query_exponents.T, output_gradient, query_clip_words)

    def query_specs(offset):
        def rows_of(n):
            return pl.BlockSpec((STEP, n), lambda b: (b + offset, 0))

        powers = query_width // SHARED_EXPONENT
        return [
            pl.BlockSpec(memory_space=pltpu.SMEM),
            rows_of(query_width),
            pl.BlockSpec((powers, STEP), lambda b: (0, b + offset)),
            rows_of(query_width),
            rows_of(query_width // WORD_BITS),
        ]

    def scratch(count):
        return [
            pltpu.VMEM((count, width), bf16),
            pltpu.VMEM((groups, count, head), bf16),
            pltpu.VMEM((groups, count, head), bf16),
            pltpu.VMEM((count, width), f32),
            pltpu.VMEM((count, width), f32),
            pltpu.VMEM((width // 2, LANES), f32),
            pltpu.VMEM((8, lanes), f32),
            pltpu.VMEM((8, lanes), f32),
        ]

    params = pltpu.CompilerParams(vmem_limit_bytes=67043328)
    full_q = jax.ShapeDtypeStruct((rows, query_width), bf16)
    full_k = jax.ShapeDtypeStruct((rows, width), bf16)
    edge_f = jax.ShapeDtypeStruct((WINDOW, 2 * width), f32)
    pay_f = jax.ShapeDtypeStruct((pay_rows, LANES), f32)
    grad_q, kgr, vgr, front, tail, part = pl.pallas_call(
        functools.partial(main_kernel, groups, per_group),
        grid=(rows // STEP - skip,),
        in_specs=query_specs(skip) + key_specs(rows, 0) + [whole(rot.shape)],
        out_specs=[
            pl.BlockSpec((STEP, query_width), lambda b: (b + skip, 0)),
            whole((rows, width)),
            whole((rows, width)),
            whole((WINDOW, 2 * width)),
            whole((WINDOW, 2 * width)),
            whole((pay_rows, LANES)),
        ],
        out_shape=[full_q, full_k, full_k, edge_f, edge_f, pay_f],
        scratch_shapes=scratch(rows),
        compiler_params=params,
        cost_estimate=pl.CostEstimate(
            flops=60_000_000_000, bytes_accessed=60_000_000, transcendentals=0
        ),
        name="attend",
    )(*query_args, *key_args, rot)

    anywhere = pl.BlockSpec(memory_space=pl.ANY)
    grad_q, kgr, vgr, back, pay, send = pl.pallas_call(
        functools.partial(front_kernel, groups, per_group),
        grid=(skip,),
        in_specs=query_specs(0)
        + key_specs(WINDOW, 0)
        + [
            whole(rot.shape),
            whole((WINDOW, 2 * width + LANES)),
            whole((WINDOW, 2 * width)),
            whole((pay_rows, LANES)),
            anywhere,
            anywhere,
            anywhere,
        ],
        out_specs=[
            pl.BlockSpec((STEP, query_width), lambda b: (b, 0)),
            whole((WINDOW, width)),
            whole((WINDOW, width)),
            whole((WINDOW, 2 * width)),
            whole((pay_rows, LANES)),
            whole((pay_rows, LANES)),
        ],
        out_shape=[
            full_q,
            full_k,
            full_k,
            jax.ShapeDtypeStruct((WINDOW, 2 * width), bf16),
            pay_f,
            jax.ShapeDtypeStruct((pay_rows, LANES), bf16),
        ],
        input_output_aliases={14: 0, 15: 1, 16: 2},
        scratch_shapes=scratch(2 * WINDOW),
        compiler_params=params,
        name="front",
    )(*query_args, *key_args, rot, halo, front, part, grad_q, kgr, vgr)

    pays = addends(pay, "seq", send, functools.partial(packed, width // 2))
    back = lax.ppermute(back, "seq", backward)
    kgr, vgr = pl.pallas_call(
        keys_kernel,
        grid=(1,),
        in_specs=[
            whole((WINDOW, 2 * width)),
            whole((WINDOW, 2 * width)),
            pl.BlockSpec((words, WINDOW), lambda b: (0, last)),
            whole(rot.shape),
            anywhere,
            anywhere,
        ],
        out_specs=[pl.BlockSpec((WINDOW, width), lambda b: (last, 0))] * 2,
        out_shape=[full_k, full_k],
        input_output_aliases={4: 0, 5: 1},
        cost_estimate=pl.CostEstimate(
            flops=1_000_000_000, bytes_accessed=3_000_000, transcendentals=0
        ),
        compiler_params=pltpu.CompilerParams(vmem_limit_bytes=8 * 1024 * 1024),
        name="keys",
    )(tail, back, key_words, rot, kgr, vgr)
    raw, square, sink_sum = pl.pallas_call(
        functools.partial(raw_kernel, groups),
        out_shape=[
            jax.ShapeDtypeStruct((groups, head, head), f32),
            jax.ShapeDtypeStruct((8, LANES), f32),
            jax.ShapeDtypeStruct((1, sinks.shape[0]), f32),
        ],
        compiler_params=pltpu.CompilerParams(vmem_limit_bytes=8 * 1024 * 1024),
        name="raw",
    )(rotation, *pays)
    grad_rotation = pl.pallas_call(
        functools.partial(scale_kernel, limit_value),
        out_shape=jax.ShapeDtypeStruct((groups, head, head), f32),
        compiler_params=pltpu.CompilerParams(vmem_limit_bytes=8 * 1024 * 1024),
        name="scale",
    )(raw, *addends(square, "head"))
    return (
        grad_q,
        kgr[:, :real_width],
        vgr[:, :real_width],
        grad_rotation,
        sink_sum.reshape(-1),
    )


def solution(mesh):
    return jax.shard_map(
        device_work,
        mesh=mesh,
        in_specs=(
            P("seq", "head"),
            P("seq", "head"),
            P("seq", "head"),
            P("seq", "head"),
            P("seq", "head"),
            P("seq", "head"),
            P("seq", "head"),
            P("seq", "head"),
            P("head"),
            P("head", None, None),
            P("seq", "head"),
        ),
        out_specs=(
            P("seq", "head"),
            P("seq", "head"),
            P("seq", "head"),
            P("head", None, None),
            P("head"),
        ),
        check_vma=False,
    )
```

```python
import functools
import math

import jax
import jax.numpy as jnp
from jax import lax
from jax.experimental import pallas as pl
from jax.experimental.pallas import tpu as pltpu
from jax.sharding import PartitionSpec as P


WINDOW = 128
SHARED_EXPONENT = 32
WORD_BITS = 16
LANES = 128
UNIT = 32
STEP = 128
BAND = WINDOW + UNIT
AHEAD = 2
LAG = 3

clip_scale = 64.0
limit_factor = 0.05
negative = -1e30

f32 = jnp.float32
bf16 = jnp.bfloat16
i32 = jnp.int32


def iota(shape, dim):
    return lax.broadcasted_iota(i32, shape, dim)


def mm(a, b):
    return lax.dot_general(a, b, (((1,), (0,)), ((), ())), preferred_element_type=f32)


def mm_nt(a, b):
    return lax.dot_general(a, b, (((1,), (1,)), ((), ())), preferred_element_type=f32)


def mm_tn(a, b):
    return lax.dot_general(a, b, (((0,), (0,)), ((), ())), preferred_element_type=f32)


def zero_one(mask):
    return mask.astype(f32).astype(bf16)


def decoded(elements, powers):
    shape = (powers.shape[0], elements.shape[1])
    spread = zero_one(iota(shape, 1) // SHARED_EXPONENT == iota(shape, 0))
    scale = mm_tn(jnp.exp2(powers.astype(f32)).astype(bf16), spread)
    return elements * scale.astype(bf16)


def word_bytes(words):
    count = words.shape[0]
    shape = (count, LANES)
    low = zero_one(iota(shape, 1) == iota(shape, 0))
    high = zero_one(iota(shape, 1) == iota(shape, 0) + count)
    first = (words & 255).astype(f32).astype(bf16)
    second = ((words >> 8) & 255).astype(f32).astype(bf16)
    return (mm_tn(first, low) + mm_tn(second, high)).astype(bf16)


def entry_flags(words):
    count, rows = words.shape
    spots = jnp.concatenate(
        [jnp.broadcast_to(words[n : n + 1], (WORD_BITS, rows)) for n in range(count)], axis=0
    )
    row = iota((count * WORD_BITS, 1), 0)
    return (spots & jnp.left_shift(jnp.ones_like(row), row % WORD_BITS)) != 0


def raw_keys(masked, rot_ref):
    head = rot_ref.shape[1]
    turned = [
        mm(rot_ref[g].astype(bf16), masked[g * head : (g + 1) * head])
        for g in range(masked.shape[0] // head)
    ]
    return jnp.transpose(jnp.concatenate(turned, axis=0).astype(bf16))


def halo_kernel(k_ref, ke_ref, v_ref, ve_ref, w_ref, out_ref):
    width = k_ref.shape[1]
    out_ref[:, :width] = decoded(k_ref[...], ke_ref[...])
    out_ref[:, width : 2 * width] = decoded(v_ref[...], ve_ref[...])
    out_ref[:, 2 * width :] = word_bytes(w_ref[...])


def attend_step(groups, per_group, edge, refs, scratch):
    _, q_ref, qe_ref, do_ref, qw_ref, rot_ref, gq_ref = refs
    kn, kg, vg, acck, accv, accp, accs, sinks = scratch
    b = pl.program_id(0)
    side = per_group // 2
    half_lanes = side * UNIT
    lanes = 2 * half_lanes
    head = LANES // 2
    start = pl.multiple_of(b * STEP, STEP)
    words = jnp.transpose(qw_ref[...])
    scales = jnp.exp2(qe_ref[...].astype(f32))
    column = iota((UNIT, lanes), 1) % UNIT
    current = iota((UNIT, lanes), 0) <= column
    low = zero_one(iota((UNIT, lanes), 0) > column)
    bit = jnp.left_shift(jnp.ones((head, 1), i32), iota((head, 1), 0) % WORD_BITS)
    per_pair = 2 * head // WORD_BITS
    per_scale = 2 * head // SHARED_EXPONENT
    shared = {}

    def turned_tile(ref, g, s):
        rows = [
            ref[s * UNIT : (s + 1) * UNIT, (side * g + p) * LANES : (side * g + p + 1) * LANES]
            for p in range(side)
        ]
        both = jnp.transpose(jnp.concatenate(rows, axis=0))
        return jnp.concatenate([both[:head], both[head:]], axis=1)

    def side_by_side(x, base, count, s):
        return jnp.concatenate(
            [
                x[base + p * count : base + (p + 1) * count, s * UNIT : (s + 1) * UNIT]
                for p in range(side)
            ],
            axis=1,
        )

    def operands(g, s):
        if (g, s) not in shared:
            scale = side_by_side(scales, g * side * per_scale, per_scale, s)
            each = per_scale // 2
            scale = jnp.concatenate(
                [
                    jnp.concatenate(
                        [
                            jnp.broadcast_to(
                                scale[odd * each + n : odd * each + n + 1],
                                (SHARED_EXPONENT, half_lanes),
                            )
                            for n in range(each)
                        ],
                        axis=0,
                    )
                    for odd in range(2)
                ],
                axis=1,
            )
            qt = turned_tile(q_ref, g, s) * scale.astype(bf16)
            shared[g, s] = (qt, turned_tile(do_ref, g, s))
        return shared[g, s]

    def band(s):
        return pl.ds(start + s * UNIT, BAND)

    def combined(x):
        mid = x[UNIT:WINDOW]
        return jnp.concatenate([jnp.where(current, x[WINDOW:], x[:UNIT]), mid], axis=0)

    def spread(x):
        first = x[:UNIT] * low
        return jnp.concatenate([first, x[UNIT:], x[:UNIT] - first], axis=0)

    def fetch(g, s):
        operands(g, s)
        if ("k", g // 2, s) not in shared:
            at = (g // 2) * LANES
            shared["k", g // 2, s] = jnp.transpose(kn[band(s), at : at + LANES])
        spots = side_by_side(words, g * side * per_pair, per_pair, s)
        return kg[g, band(s), :], vg[g, band(s), :], sinks[pl.ds(g, 1), :], spots

    def scores_of(g, s, loaded):
        scores = mm(loaded[0], operands(g, s)[0])
        if edge:
            limit = jnp.where(lax.axis_index("seq") == 0, WINDOW, 0) - (start + s * UNIT)
            scores = jnp.where(iota((BAND, 1), 0) >= limit, scores, negative)
        return combined(scores)

    def gprobs_of(g, s, loaded):
        return combined(mm(loaded[1], operands(g, s)[1]))

    def soft(g, s, loaded, scores, gprobs):
        sink = loaded[2]
        row_max = jnp.maximum(jnp.max(scores, axis=0, keepdims=True), sink)
        numer = jnp.exp(scores - row_max)
        sink_numer = jnp.exp(sink - row_max)
        inverse = 1.0 / (jnp.sum(numer, axis=0, keepdims=True) + sink_numer)
        weights = numer * inverse
        delta = jnp.sum(weights * gprobs, axis=0, keepdims=True)
        gscores = (weights * (gprobs - delta)).astype(bf16)
        term = sink_numer * inverse * delta
        return spread(weights.astype(bf16)), spread(gscores), term

    def grad_query(g, s, grads):
        return mm(shared["k", g // 2, s][(g % 2) * head : (g % 2 + 1) * head], grads)

    def grad_keys(g, s, grads):
        return in_window(mm_nt(operands(g, s)[0], grads), s)

    def grad_values(g, s, probs):
        return in_window(mm_nt(operands(g, s)[1], probs), s)

    def in_window(x, s):
        before, after = s * UNIT, STEP - UNIT - s * UNIT
        zeros = [jnp.zeros((head, n), f32) for n in (before, after)]
        parts = [zeros[0]] * (before > 0) + [x] + [zeros[1]] * (after > 0)
        return jnp.concatenate(parts, axis=1)

    def clipped(g, s, loaded, dq):
        spots = loaded[3]
        each = per_pair // 2
        spots = jnp.concatenate(
            [
                jnp.concatenate(
                    [
                        jnp.broadcast_to(
                            spots[odd * each + n : odd * each + n + 1], (WORD_BITS, half_lanes)
                        )
                        for n in range(each)
                    ],
                    axis=0,
                )
                for odd in range(2)
            ],
            axis=1,
        )
        return jnp.where((spots & bit) != 0, dq, 0.0).astype(bf16)

    def turned_back(g, s, masked):
        turned = mm(rot_ref[g].astype(bf16), masked).astype(bf16)
        return jnp.concatenate([turned[:, :half_lanes], turned[:, half_lanes:]], axis=0)

    def rotation_term(g, s, masked):
        return mm_nt(masked, operands(g, s)[0])

    sums = {}

    def finish(g, s, term, turned, *parts):
        turned = jnp.transpose(turned)
        for p in range(side):
            cols = (side * g + p) * LANES
            gq_ref[s * UNIT : (s + 1) * UNIT, cols : cols + LANES] = turned[
                p * UNIT : (p + 1) * UNIT
            ]
        accs[pl.ds(g, 1), :] -= term
        if s:
            parts = tuple(x + y for x, y in zip(sums[g], parts))
        sums[g] = parts
        if s + 1 < STEP // UNIT:
            return
        window = pl.ds(start, WINDOW + STEP)
        mine = slice(g * head, (g + 1) * head)
        acck[mine, window] += parts[0]
        accv[mine, window] += parts[1]
        accp[mine] += parts[2]

    units = [
        (g, s)
        for pair in range((groups + 1) // 2)
        for s in range(STEP // UNIT)
        for g in (2 * pair, 2 * pair + 1)
        if g < groups
    ]
    loaded, scores, gprobs, soft_out, masked, turned = ({} for _ in range(6))
    dk, dv, dp = {}, {}, {}
    wide = 2
    teams = [range(n, min(n + wide, len(units))) for n in range(0, len(units), wide)]

    def stage(n, lead):
        n += lead
        return teams[n] if 0 <= n < len(teams) else ()

    for turn in range(-AHEAD, len(teams) + LAG):
        for n in stage(turn, AHEAD):
            loaded[n] = fetch(*units[n])
        for n in stage(turn, -1):
            masked[n] = clipped(*units[n], loaded[n], grad_query(*units[n], soft_out[n][1]))
        for n in stage(turn, 1):
            scores[n] = scores_of(*units[n], loaded[n])
        for n in stage(turn, -1):
            dk[n] = grad_keys(*units[n], soft_out[n][1])
        for n in stage(turn, 1):
            gprobs[n] = gprobs_of(*units[n], loaded[n])
        for n in stage(turn, -1):
            dv[n] = grad_values(*units[n], soft_out[n][0])
        for n in stage(turn, -2):
            turned[n] = turned_back(*units[n], masked[n])
        for n in stage(turn, -2):
            dp[n] = rotation_term(*units[n], masked[n])
        for n in stage(turn, 0):
            soft_out[n] = soft(*units[n], loaded[n], scores.pop(n), gprobs.pop(n))
        for n in stage(turn, -LAG):
            finish(*units[n], soft_out[n][2], turned[n], dk[n], dv[n], dp[n])


def prepare(groups, per_group, sink_ref, keys, values, scratch):
    kn, kg, vg, _, _, _, accs, sinks = scratch
    head = LANES // 2
    side = per_group // 2
    eighth = jnp.asarray(head**-0.5, bf16)
    for at, k, v in zip((0, WINDOW), keys, values):
        k = k * eighth
        kn[at : at + k.shape[0]] = k
        for g in range(groups):
            kg[g, at : at + k.shape[0]] = k[:, g * head : (g + 1) * head]
            vg[g, at : at + k.shape[0]] = v[:, g * head : (g + 1) * head]
    lanes = per_group * UNIT
    block = iota((1, lanes), 1) // UNIT
    for g in range(groups):
        row = jnp.zeros((1, lanes), f32)
        for n in range(per_group):
            h = 2 * (n % side) + n // side
            row = jnp.where(block == n, sink_ref[g * per_group + h], row)
        sinks[pl.ds(g, 1), :] = row
    accs[...] = jnp.zeros_like(accs)


def sink_sums(groups, per_group, accs):
    side = per_group // 2
    shape = (accs.shape[0], LANES)
    row, lane = iota(shape, 0), iota(shape, 1)
    total = jnp.zeros(shape, f32)
    for n in range(per_group):
        part = jnp.sum(accs[:, n * UNIT : (n + 1) * UNIT], axis=1, keepdims=True)
        h = 2 * (n % side) + n // side
        total = total + jnp.where((lane == row * per_group + h) & (row < groups), part, 0.0)
    return jnp.sum(total, axis=0, keepdims=True)


def with_keys(gk, words, rows, scratch, pay_ref):
    _, kg, _, _, _, accp, _, _ = scratch
    head = kg.shape[2]
    masked = jnp.where(entry_flags(words), gk, 0.0).astype(bf16)
    for pair in range(gk.shape[0] // LANES):
        sums = []
        for g in (2 * pair, 2 * pair + 1):
            mine = slice(g * head, (g + 1) * head)
            total = accp[mine]
            if g < kg.shape[0]:
                total = total + mm(masked[mine], kg[g, rows, :]) * float(head) ** 0.5
            sums.append(total)
        pay_ref[pair * head : (pair + 1) * head] = jnp.concatenate(sums, axis=1)
    return masked


def main_kernel(
    groups,
    per_group,
    sink_ref,
    q_ref,
    qe_ref,
    do_ref,
    qw_ref,
    k_ref,
    ke_ref,
    v_ref,
    ve_ref,
    kw_ref,
    rot_ref,
    gq_ref,
    kgr_ref,
    vgr_ref,
    front_ref,
    tail_ref,
    pay_ref,
    *scratch,
):
    _, _, _, acck, accv, accp, accs, _ = scratch
    b = pl.program_id(0)
    rows, width = k_ref.shape
    head = LANES // 2

    @pl.when(b == 0)
    def _():
        keys = decoded(k_ref[...], ke_ref[...])
        values = decoded(v_ref[...], ve_ref[...])
        prepare(groups, per_group, sink_ref, (keys,), (values,), scratch)
        acck[...] = jnp.zeros_like(acck)
        accv[...] = jnp.zeros_like(accv)
        accp[...] = jnp.zeros_like(accp)

    refs = (sink_ref, q_ref, qe_ref, do_ref, qw_ref, rot_ref, gq_ref)
    attend_step(groups, per_group, False, refs, scratch)

    @pl.when(b == pl.num_programs(0) - 1)
    def _():
        front_ref[:width] = acck[:, :WINDOW]
        front_ref[width:] = accv[:, :WINDOW]
        gk = acck[:, WINDOW:] * (head**-0.5)
        gv = accv[:, WINDOW:]
        tail_ref[:width] = gk[:, rows - 2 * WINDOW :]
        tail_ref[width : 2 * width] = gv[:, rows - 2 * WINDOW :]
        tail_ref[2 * width :] = kw_ref[:, rows - WINDOW :].astype(f32)
        vgr_ref[WINDOW:] = jnp.transpose(gv.astype(bf16))
        masked = with_keys(gk, kw_ref[:, WINDOW:], pl.ds(WINDOW, rows - WINDOW), scratch, pay_ref)
        kgr_ref[WINDOW:] = raw_keys(masked, rot_ref)
        pay_ref[width // 2 :] = jnp.broadcast_to(sink_sums(groups, per_group, accs), (16, LANES))


def front_kernel(
    groups,
    per_group,
    sink_ref,
    q_ref,
    qe_ref,
    do_ref,
    qw_ref,
    k_ref,
    ke_ref,
    v_ref,
    ve_ref,
    kw_ref,
    rot_ref,
    halo_ref,
    front_ref,
    part_ref,
    gq_in,
    kgr_in,
    vgr_in,
    gq_ref,
    kgr_ref,
    vgr_ref,
    ret_ref,
    pay_ref,
    send_ref,
    *scratch,
):
    _, _, _, acck, accv, accp, accs, _ = scratch
    b = pl.program_id(0)
    width = k_ref.shape[1]
    head = LANES // 2

    @pl.when(b == 0)
    def _():
        keys = decoded(k_ref[...], ke_ref[...])
        values = decoded(v_ref[...], ve_ref[...])
        keys = (halo_ref[:, :width], keys)
        values = (halo_ref[:, width : 2 * width], values)
        prepare(groups, per_group, sink_ref, keys, values, scratch)
        acck[:, :WINDOW] = jnp.zeros((width, WINDOW), f32)
        accv[:, :WINDOW] = jnp.zeros((width, WINDOW), f32)
        acck[:, WINDOW:] = front_ref[:width]
        accv[:, WINDOW:] = front_ref[width:]
        for g in range(width // head):
            accp[g * head : (g + 1) * head] = part_ref[
                (g // 2) * head : (g // 2 + 1) * head, (g % 2) * head : (g % 2 + 1) * head
            ]

    refs = (sink_ref, q_ref, qe_ref, do_ref, qw_ref, rot_ref, gq_ref)
    attend_step(groups, per_group, True, refs, scratch)

    @pl.when(b == pl.num_programs(0) - 1)
    def _():
        gk = acck[...] * (head**-0.5)
        gv = accv[...].astype(bf16)
        ret_ref[:width] = gk[:, :WINDOW].astype(bf16)
        ret_ref[width:] = gv[:, :WINDOW]
        vgr_ref[...] = jnp.transpose(gv[:, WINDOW:])
        count = width // WORD_BITS
        pieces = jnp.transpose(halo_ref[:, 2 * width :]).astype(f32)
        words = (pieces[:count] + 256.0 * pieces[count : 2 * count]).astype(i32)
        words = jnp.concatenate([words, kw_ref[...]], axis=1)
        masked = with_keys(gk, words, slice(None), scratch, pay_ref)
        kgr_ref[...] = raw_keys(masked[:, WINDOW:], rot_ref)
        sink = part_ref[width // 2 : width // 2 + 1] + sink_sums(groups, per_group, accs)
        tail_row = iota((16, LANES), 0)
        pay_ref[width // 2 :] = jnp.where(tail_row == 0, sink, 0.0)
        send_ref[: width // 2] = pay_ref[: width // 2].astype(bf16)
        rest = sink - sink.astype(bf16).astype(f32)
        send_ref[width // 2 :] = jnp.where(
            tail_row == 0, sink, jnp.where(tail_row == 1, rest, 0.0)
        ).astype(bf16)


def keys_kernel(tail_ref, back_ref, rot_ref, kgr_in, vgr_in, kgr_ref, vgr_ref):
    width = kgr_ref.shape[1]
    both = tail_ref[: 2 * width] + back_ref[...].astype(f32)
    flags = entry_flags(tail_ref[2 * width :].astype(i32))
    masked = jnp.where(flags, both[:width], 0.0).astype(bf16)
    kgr_ref[...] = raw_keys(masked, rot_ref)
    vgr_ref[...] = jnp.transpose(both[width:].astype(bf16))


def raw_kernel(groups, rot_ref, *refs):
    *pays, raw_ref, sq_ref, sink_ref = refs
    head = LANES // 2
    pay = pays[0][...]
    for x in pays[1:]:
        pay = pay + x[...].astype(f32)
    total = jnp.zeros((1, head), f32)
    for g in range(groups):
        part = pay[(g // 2) * head : (g // 2 + 1) * head, (g % 2) * head : (g % 2 + 1) * head]
        raw = lax.dot_general(
            rot_ref[g],
            part,
            (((1,), (1,)), ((), ())),
            precision=lax.Precision.HIGHEST,
            preferred_element_type=f32,
        )
        raw_ref[g] = raw
        total = total + jnp.sum(raw * raw, axis=0, keepdims=True)
    sq_ref[...] = jnp.broadcast_to(jnp.sum(total, axis=1, keepdims=True), sq_ref.shape)
    at = pay.shape[0] - 16
    sink_ref[...] = (pay[at : at + 1] + pay[at + 1 : at + 2])[:, : sink_ref.shape[1]]


def scale_kernel(limit_value, raw_ref, *refs):
    *squares, out_ref = refs
    square = squares[0][:1, :1]
    for x in squares[1:]:
        square = square + x[:1, :1]
    factor = clip_scale / jnp.maximum(jnp.sqrt(square), limit_value)
    for g in range(raw_ref.shape[0]):
        out_ref[g] = raw_ref[g] * factor


def addends(x, axis, send=None, pack=None):
    size = lax.axis_size(axis)
    if size & (size - 1):
        return [lax.psum(x, axis)]
    step, parts = 1, [x]
    while step < size:
        if step > 1:
            x = functools.reduce(jnp.add, [part.astype(f32) for part in parts])
            send = None if pack is None else pack(x)
        masks = (3 * step, 2 * step, step) if 2 * step < size else (step,)
        swaps = [[(i, i ^ m) for i in range(size)] for m in masks]
        out = x if send is None else send
        parts = [x]
        for swap in swaps:
            parts.append(lax.ppermute(out, axis, swap))
        step *= 4
    return parts


def packed(rows, x):
    rest = x - lax.reduce_precision(x, 8, 7)
    moved = jnp.concatenate([rest[-1:], rest[:-1]], axis=0)
    row = iota(x.shape, 0)
    return jnp.where(row == rows + 1, x + moved, x).astype(bf16)


def whole(shape):
    return pl.BlockSpec(shape, lambda *_: (0,) * len(shape))


def device_work(
    query_elements,
    query_exponents,
    key_elements,
    key_exponents,
    value_elements,
    value_exponents,
    query_clip_words,
    key_clip_words,
    sinks,
    rotation,
    output_gradient,
):
    rows, query_width = query_elements.shape
    groups, head, _ = rotation.shape
    per_group = sinks.shape[0] // groups
    real_width = groups * head
    padded = groups + groups % 2
    width = padded * head
    rot = rotation
    key_powers, value_powers = key_exponents.T, value_exponents.T
    key_words = key_clip_words.T
    if padded != groups:
        spare = width - real_width
        key_elements = jnp.pad(key_elements, ((0, 0), (0, spare)))
        value_elements = jnp.pad(value_elements, ((0, 0), (0, spare)))
        key_powers = jnp.pad(key_powers, ((0, spare // SHARED_EXPONENT), (0, 0)))
        value_powers = jnp.pad(value_powers, ((0, spare // SHARED_EXPONENT), (0, 0)))
        key_words = jnp.pad(key_words, ((0, spare // WORD_BITS), (0, 0)))
        rot = jnp.pad(rotation, ((0, padded - groups), (0, 0), (0, 0)))
    lanes = per_group * UNIT
    blocks = width // SHARED_EXPONENT
    words = width // WORD_BITS
    all_tokens = rows * lax.axis_size("seq")
    all_heads = sinks.shape[0] * lax.axis_size("head")
    limit_value = limit_factor * math.sqrt(all_tokens * all_heads * head)
    devices = range(lax.axis_size("seq"))
    forward = [(i - 1, i) for i in devices if i]
    backward = [(i, i - 1) for i in devices if i]
    key_args = (key_elements, key_powers, value_elements, value_powers, key_words)

    def key_specs(count, index):
        return [
            pl.BlockSpec((count, width), lambda *_: (index, 0)),
            pl.BlockSpec((blocks, count), lambda *_: (0, index)),
            pl.BlockSpec((count, width), lambda *_: (index, 0)),
            pl.BlockSpec((blocks, count), lambda *_: (0, index)),
            pl.BlockSpec((words, count), lambda *_: (0, index)),
        ]

    last = rows // WINDOW - 1
    halo = pl.pallas_call(
        halo_kernel,
        grid=(1,),
        in_specs=key_specs(WINDOW, last),
        out_specs=whole((WINDOW, 2 * width + LANES)),
        out_shape=jax.ShapeDtypeStruct((WINDOW, 2 * width + LANES), bf16),
        name="halo",
    )(*key_args)
    halo = lax.ppermute(halo, "seq", forward)

    def in_hbm(args):
        return [pltpu.with_memory_space_constraint(x, pltpu.HBM) for x in args]

    skip = WINDOW // STEP
    pay_rows = width // 2 + 16
    query_args = (sinks, query_elements, query_exponents.T, output_gradient, query_clip_words)

    def query_specs(offset):
        def rows_of(n):
            return pl.BlockSpec((STEP, n), lambda b: (b + offset, 0))

        powers = query_width // SHARED_EXPONENT
        return [
            pl.BlockSpec(memory_space=pltpu.SMEM),
            rows_of(query_width),
            pl.BlockSpec((powers, STEP), lambda b: (0, b + offset)),
            rows_of(query_width),
            rows_of(query_width // WORD_BITS),
        ]

    def scratch(count):
        return [
            pltpu.VMEM((count, width), bf16),
            pltpu.VMEM((groups, count, head), bf16),
            pltpu.VMEM((groups, count, head), bf16),
            pltpu.VMEM((width, count), f32),
            pltpu.VMEM((width, count), f32),
            pltpu.VMEM((width, head), f32),
            pltpu.VMEM((8, lanes), f32),
            pltpu.VMEM((8, lanes), f32),
        ]

    params = pltpu.CompilerParams(vmem_limit_bytes=40 * 1024 * 1024)
    full_q = jax.ShapeDtypeStruct((rows, query_width), bf16)
    full_k = jax.ShapeDtypeStruct((rows, width), bf16)
    edge_f = jax.ShapeDtypeStruct((2 * width, WINDOW), f32)
    tail_f = jax.ShapeDtypeStruct((2 * width + words, WINDOW), f32)
    pay_f = jax.ShapeDtypeStruct((pay_rows, LANES), f32)
    grad_q, kgr, vgr, front, tail, part = pl.pallas_call(
        functools.partial(main_kernel, groups, per_group),
        grid=(rows // STEP - skip,),
        in_specs=query_specs(skip) + key_specs(rows, 0) + [whole(rot.shape)],
        out_specs=[
            pl.BlockSpec((STEP, query_width), lambda b: (b + skip, 0)),
            whole((rows, width)),
            whole((rows, width)),
            whole((2 * width, WINDOW)),
            whole((2 * width + words, WINDOW)),
            whole((pay_rows, LANES)),
        ],
        out_shape=[full_q, full_k, full_k, edge_f, tail_f, pay_f],
        scratch_shapes=scratch(rows),
        compiler_params=params,
        cost_estimate=pl.CostEstimate(
            flops=60_000_000_000, bytes_accessed=60_000_000, transcendentals=0
        ),
        name="attend",
    )(*in_hbm((*query_args, *key_args, rot)))

    anywhere = pl.BlockSpec(memory_space=pl.ANY)
    grad_q, kgr, vgr, back, pay, send = pl.pallas_call(
        functools.partial(front_kernel, groups, per_group),
        grid=(skip,),
        in_specs=query_specs(0)
        + key_specs(WINDOW, 0)
        + [
            whole(rot.shape),
            whole((WINDOW, 2 * width + LANES)),
            whole((2 * width, WINDOW)),
            whole((pay_rows, LANES)),
            anywhere,
            anywhere,
            anywhere,
        ],
        out_specs=[
            pl.BlockSpec((STEP, query_width), lambda b: (b, 0)),
            whole((WINDOW, width)),
            whole((WINDOW, width)),
            whole((2 * width, WINDOW)),
            whole((pay_rows, LANES)),
            whole((pay_rows, LANES)),
        ],
        out_shape=[
            full_q,
            full_k,
            full_k,
            jax.ShapeDtypeStruct((2 * width, WINDOW), bf16),
            pay_f,
            jax.ShapeDtypeStruct((pay_rows, LANES), bf16),
        ],
        input_output_aliases={14: 0, 15: 1, 16: 2},
        scratch_shapes=scratch(2 * WINDOW),
        compiler_params=params,
        name="front",
    )(
        *in_hbm((*query_args, *key_args, rot)),
        halo,
        front,
        part,
        grad_q,
        kgr,
        vgr,
    )

    pays = addends(pay, "seq", send, functools.partial(packed, width // 2))
    back = lax.ppermute(back, "seq", backward)
    kgr, vgr = pl.pallas_call(
        keys_kernel,
        grid=(1,),
        in_specs=[
            whole((2 * width + words, WINDOW)),
            whole((2 * width, WINDOW)),
            whole(rot.shape),
            anywhere,
            anywhere,
        ],
        out_specs=[pl.BlockSpec((WINDOW, width), lambda b: (last, 0))] * 2,
        out_shape=[full_k, full_k],
        input_output_aliases={3: 0, 4: 1},
        cost_estimate=pl.CostEstimate(
            flops=1_000_000_000, bytes_accessed=3_000_000, transcendentals=0
        ),
        compiler_params=pltpu.CompilerParams(vmem_limit_bytes=8 * 1024 * 1024),
        name="keys",
    )(tail, back, rot, kgr, vgr)
    raw, square, sink_sum = pl.pallas_call(
        functools.partial(raw_kernel, groups),
        out_shape=[
            jax.ShapeDtypeStruct((groups, head, head), f32),
            jax.ShapeDtypeStruct((8, LANES), f32),
            jax.ShapeDtypeStruct((1, sinks.shape[0]), f32),
        ],
        compiler_params=pltpu.CompilerParams(vmem_limit_bytes=8 * 1024 * 1024),
        name="raw",
    )(rot, *pays)
    grad_rotation = pl.pallas_call(
        functools.partial(scale_kernel, limit_value),
        out_shape=jax.ShapeDtypeStruct((groups, head, head), f32),
        compiler_params=pltpu.CompilerParams(vmem_limit_bytes=8 * 1024 * 1024),
        name="scale",
    )(raw, *addends(square, "head"))
    return (
        grad_q,
        kgr[:, :real_width],
        vgr[:, :real_width],
        grad_rotation,
        sink_sum.reshape(-1),
    )


def solution(mesh):
    return jax.shard_map(
        device_work,
        mesh=mesh,
        in_specs=(
            P("seq", "head"),
            P("seq", "head"),
            P("seq", "head"),
            P("seq", "head"),
            P("seq", "head"),
            P("seq", "head"),
            P("seq", "head"),
            P("seq", "head"),
            P("head"),
            P("head", None, None),
            P("seq", "head"),
        ),
        out_specs=(
            P("seq", "head"),
            P("seq", "head"),
            P("seq", "head"),
            P("head", None, None),
            P("head"),
        ),
        check_vma=False,
    )
```
